128 devices in a mesh: section: 16 (over y_lo, z, core), dp: 8 (over x, y_hi).
Axes of the slice: x: 4, y: 4 (y_hi: 2, y_lo: 2; y = y_hi * 2 + y_lo), z: 4, core: 2. Of those that a mesh axis runs over, the one named last changes fastest.
Arguments:
- first_acts: bfloat16 [16, 1024, 8192], P('section', 'dp'), may hold values from -6 to 6
- first_grads: bfloat16 [16, 1024, 8192], P('section', 'dp'), may hold values from -6 to 6
- last_acts: bfloat16 [16, 1024, 8192], P('section', 'dp'), may hold values from -6 to 6
- last_grads: bfloat16 [16, 1024, 8192], P('section', 'dp'), may hold values from -6 to 6
- doc_lengths: int32 [8, 16], P('dp'), may hold values from 1 to 32, 128 in all within a row
- block_owner: int32 [16], replicated, may hold values from 0 to 7, as said below
Outputs:
- act_factor: float32 [16, 8, 4, 512, 512], P('section', 'dp')
- grad_factor: float32 [16, 8, 4, 512, 512], P('section', 'dp')
- act_cross: float32 [16, 8, 4, 512, 512], P('section', 'dp')
- grad_cross: float32 [16, 8, 4, 512, 512], P('section', 'dp')
The draws below stay inside these ranges and needn't reach their ends.
Inputs may be any that keep to these rules, and one draw needn't show every extreme that they name: `doc_lengths`: documents fill their group's 128 rows exactly and the longest is exactly 32 rows. `block_owner`: one owner holds exactly 4 blocks, one holds none, every other holds exactly 2; which ones is drawn, except that the first and the last group always own blocks.
All inputs are finite; a program needn't handle non-finite values.
Results may differ from the reference program's by a relative error of at most 0.0037.
Values may be sent and summed in bfloat16 or wider, within the bound.
No kernel may reach another device: no remote copies, remote signals or barrier semaphores. Data moves between devices by JAX's collectives and lax.ppermute only.
A program may use at most 320 MiB of HBM per device.

```python
import math
import jax
import jax.numpy as jnp
import numpy as np
from jax import lax

D = 8192
FB = 512
TOK_DEV = 128
DOCS = 16
SECTIONS = 16
GROUPS = 8
TOKENS = 1024
TOTAL_DOCS = 128
DOC_MOST = 32
BLOCKS = 16
OWNED = 2
MOST_OWNED = 4


def draw_block_owner(key, part):
    owners = BLOCKS // OWNED
    pattern = np.concatenate([np.zeros(MOST_OWNED, dtype=np.int32), np.repeat(np.arange(2, owners, dtype=np.int32), OWNED)])
    ranking = jax.random.permutation(jax.random.fold_in(key, 11), owners).astype(jnp.int32)
    middle_one = (ranking[1] > 0) & (ranking[1] < owners - 1)
    middle_two = (ranking[2] > 0) & (ranking[2] < owners - 1)
    pick = jnp.where(middle_one, 1, jnp.where(middle_two, 2, 3)).astype(jnp.int32)
    value_one = ranking[1]
    value_pick = ranking[pick]
    ranking = ranking.at[pick].set(value_one)
    ranking = ranking.at[1].set(value_pick)
    shuffle = jax.random.permutation(jax.random.fold_in(key, 12), BLOCKS)
    return ranking[jnp.asarray(pattern)[shuffle]].astype(jnp.int32)


def block_levels(own_key, shape, pieces, smallest, largest):
    def one(axis_at, blocks):
        draws = jax.random.uniform(jax.random.fold_in(jax.random.fold_in(own_key, 6), axis_at), (blocks,), jnp.float32, smallest / len(pieces), largest / len(pieces))
        return jnp.repeat(jnp.exp(draws), shape[axis_at] // blocks).reshape((-1,) + (1,) * (len(shape) - axis_at - 1))

    gain = one(*pieces[0])
    for cut in pieces[1:]:
        gain = gain * one(*cut)
    return gain


def length_profile(count, total, most, skew):
    loads = [(1 << 20) // math.isqrt(grade ** skew) + 1 for grade in range(2, count + 1)]
    spare, counts = total - most - (count - 1), [1] * (count - 1)
    while spare > 0:
        candidates = [i for i in range(count - 1) if counts[i] < most]
        whole, budget = sum([loads[i] for i in candidates]), spare
        for i in candidates:
            addition = min(most - counts[i], max(1, budget * loads[i] // whole), spare)
            counts[i] = counts[i] + addition
            spare = spare - addition
    return np.array([most] + counts)


def uneven(key, number_of, total, reach, lean):
    if number_of == 2:
        one = jax.random.randint(key, (), max(1, total - reach), min(reach, total - 1) + 1)
        return jnp.stack([one, total - one])
    tallies = jnp.asarray(length_profile(number_of, total, reach, lean), jnp.int32)
    twos = (number_of - 1) // 2
    giver, receiver = tallies[1:1 + 2 * twos:2], tallies[2:2 + 2 * twos:2]
    room = jnp.minimum(giver - 1, reach - receiver)
    shifted = jax.random.randint(jax.random.fold_in(key, 1), (twos,), 0, 1 << 20) % (room + 1)
    tallies = tallies.at[1:1 + 2 * twos:2].set(giver - shifted).at[2:2 + 2 * twos:2].set(receiver + shifted)
    return tallies[jax.random.permutation(jax.random.fold_in(key, 2), number_of)]


def gaussian(own_key, dims, width, bound, split=(), kind=jnp.bfloat16):
    array = width * jax.random.normal(own_key, dims, jnp.float32)
    if split:
        array = array * block_levels(own_key, dims, split, -0.22, 0.18)
    return jnp.clip(array, -bound, bound).astype(kind)


def setup_inputs(seed: int = 0) -> dict:
    splits = jax.random.split(jax.random.key(seed), 7)
    first_acts = gaussian(splits[0], (SECTIONS, TOKENS, D), 1.0, 6.0, ((0, 16), (1, 8)))
    first_grads = gaussian(splits[1], (SECTIONS, TOKENS, D), 1.0, 6.0, ((0, 16), (1, 8)))
    last_acts = gaussian(splits[2], (SECTIONS, TOKENS, D), 1.0, 6.0, ((0, 16), (1, 8)))
    last_grads = gaussian(splits[3], (SECTIONS, TOKENS, D), 1.0, 6.0, ((0, 16), (1, 8)))
    doc_lengths = jax.vmap(lambda own: uneven(own, DOCS, TOK_DEV, DOC_MOST, 2))(jax.random.split(splits[4], GROUPS)).reshape((GROUPS, DOCS)).astype(jnp.int32)
    block_owner = draw_block_owner(jax.random.fold_in(splits[6], 71), 0)
    return dict(first_acts=first_acts, first_grads=first_grads, last_acts=last_acts, last_grads=last_grads, doc_lengths=doc_lengths, block_owner=block_owner)


def row_scale(doc_lengths):
    doc_sizes = doc_lengths.astype(jnp.float32)
    doc_end = jnp.cumsum(doc_lengths, axis=1)
    starts = doc_end - doc_lengths
    places = jnp.arange(TOK_DEV, dtype=jnp.int32)
    inside = (places[None, :, None] >= starts[:, None, :]) & (places[None, :, None] < doc_end[:, None, :])
    inverse = lax.optimization_barrier(jnp.sum(jnp.where(inside, 1.0 / doc_sizes[:, None, :], jnp.float32(0.0)), axis=2))
    return jnp.sqrt(inverse / TOTAL_DOCS).reshape(TOKENS)

def slot_order(block_owner):
    position = jnp.arange(BLOCKS, dtype=jnp.int32)
    same_owner = block_owner[:, None] == block_owner[None, :]
    earlier = position[None, :] < position[:, None]
    return lax.optimization_barrier(jnp.sum(jnp.where(same_owner & earlier, 1, 0), axis=1)).astype(jnp.int32)

def block_grams(former, latter):
    first_rows = former.astype(jnp.float32).reshape(TOKENS, BLOCKS, FB)
    second_rows = latter.astype(jnp.float32).reshape(TOKENS, BLOCKS, FB)
    return jnp.einsum('tbf,tbg->bfg', first_rows, second_rows, precision=lax.Precision.HIGHEST)

def place_slots(grams, block_owner, slot_index):
    empty = jnp.zeros((GROUPS, MOST_OWNED, FB, FB), jnp.float32)
    return empty.at[block_owner, slot_index].set(grams)

def reference(first_acts, first_grads, last_acts, last_grads, doc_lengths, block_owner):
    row_weight = row_scale(doc_lengths)[:, None]
    slot_index = slot_order(block_owner)

    def weighted(matrix):
        return (matrix.astype(jnp.float32) * row_weight).astype(jnp.bfloat16)

    def one_section(section_index):
        before = jnp.maximum(section_index - 1, 0)
        has_prev = jnp.where(section_index > 0, 1.0, 0.0).astype(jnp.float32)
        own_acts = weighted(first_acts[section_index])
        own_grads = weighted(first_grads[section_index])
        prev_acts = weighted(last_acts[before])
        prev_grads = weighted(last_grads[before])
        first = place_slots(block_grams(own_acts, own_acts), block_owner, slot_index)
        second = place_slots(block_grams(own_grads, own_grads), block_owner, slot_index)
        third = place_slots(block_grams(prev_acts, own_acts), block_owner, slot_index) * has_prev
        fourth = place_slots(block_grams(prev_grads, own_grads), block_owner, slot_index) * has_prev
        return (first, second, third, fourth)
    act_factor, grad_factor, act_cross, grad_cross = lax.map(one_section, jnp.arange(SECTIONS, dtype=jnp.int32))
    return (act_factor, grad_factor, act_cross, grad_cross)
```

```python
import functools

import jax
import jax.numpy as jnp
from jax import lax
from jax.experimental import pallas as pl
from jax.experimental.pallas import tpu as pltpu
from jax.sharding import PartitionSpec as P

FB = 512
KEEP = 2


def row_scale(doc_lengths, row_count, docs_all):
    doc_sizes = doc_lengths.astype(jnp.float32)
    doc_end = jnp.cumsum(doc_lengths)
    starts = doc_end - doc_lengths
    places = jnp.arange(row_count, dtype=jnp.int32)
    inside = (places[:, None] >= starts[None, :]) & (places[:, None] < doc_end[None, :])
    inverse = jnp.sum(jnp.where(inside, 1.0 / doc_sizes[None, :], jnp.float32(0.0)), axis=1)
    return jnp.sqrt(inverse / docs_all)


def placement(block_owner, groups):
    blocks = block_owner.shape[0]
    position = jnp.arange(blocks, dtype=jnp.int32)
    same_owner = block_owner[:, None] == block_owner[None, :]
    slot = jnp.sum(jnp.where(same_owner & (position[None, :] < position[:, None]), 1, 0), axis=1)
    owned = jnp.sum(jnp.where(block_owner[:, None] == jnp.arange(groups)[None, :], 1, 0), axis=0)
    group = jnp.arange(groups, dtype=jnp.int32)
    spare = jnp.sum(jnp.where(owned == 0, group, 0))
    full = jnp.sum(jnp.where(owned > KEEP, group, 0))
    target = jnp.where(slot < KEEP, block_owner, spare) * KEEP + slot % KEEP
    order = jnp.sum(jnp.where(target[None, :] == position[:, None], position[None, :], 0), axis=1)
    return order.astype(jnp.int32), spare.astype(jnp.int32), full.astype(jnp.int32)


def scale_kernel(order, weight, fa, fg, la, lg, f_out, la_out, lg_out):
    w = weight[...]

    def scaled(ref):
        return (ref[...].astype(jnp.float32) * w).astype(jnp.bfloat16)

    f_out[0, 0, 0] = scaled(fa)
    f_out[0, 1, 0] = scaled(fg)
    la_out[0, 0] = scaled(la)
    lg_out[0, 0] = scaled(lg)


def scale_and_sort(order, weight, fa, fg, la, lg, groups):
    rows = fa.shape[0]
    blocks = groups * KEEP
    column = pl.BlockSpec((rows, FB), lambda i, o: (0, o[i]))
    return pl.pallas_call(
        scale_kernel,
        grid_spec=pltpu.PrefetchScalarGridSpec(
            num_scalar_prefetch=1,
            grid=(blocks,),
            in_specs=[pl.BlockSpec((rows, 1), lambda i, o: (0, 0))] + [column] * 4,
            out_specs=[
                pl.BlockSpec((1, 2, 1, rows, FB), lambda i, o: (i // KEEP, 0, i % KEEP, 0, 0)),
                pl.BlockSpec((1, 1, rows, FB), lambda i, o: (i // KEEP, i % KEEP, 0, 0)),
                pl.BlockSpec((1, 1, rows, FB), lambda i, o: (i // KEEP, i % KEEP, 0, 0)),
            ],
        ),
        out_shape=[
            jax.ShapeDtypeStruct((groups, 2, KEEP, rows, FB), jnp.bfloat16),
            jax.ShapeDtypeStruct((groups, KEEP, rows, FB), jnp.bfloat16),
            jax.ShapeDtypeStruct((groups, KEEP, rows, FB), jnp.bfloat16),
        ],
        name="scale_sort",
    )(order, weight, fa, fg, la, lg)


def gram(x, y):
    return lax.dot_general(x, y, (((0,), (0,)), ((), ())), preferred_element_type=jnp.float32)


def factor_kernel(mine, f_in, a_out, g_out, hand):
    k = pl.program_id(0)

    @pl.when(k < KEEP)
    def _():
        keep = mine[0] != 0
        for a, out in ((0, a_out), (1, g_out)):
            x = f_in[:, a, 0].reshape(-1, FB)
            r = gram(x, x)
            out[0] = jnp.where(keep, r, 0.0)
            hand[a, 0] = r.astype(jnp.bfloat16)

    @pl.when(k >= KEEP)
    def _():
        a_out[...] = jnp.zeros_like(a_out)
        g_out[...] = jnp.zeros_like(g_out)


def factors(mine, f_in):
    groups, _, _, rows, _ = f_in.shape
    out = jax.ShapeDtypeStruct((2 * KEEP, FB, FB), jnp.float32)
    return pl.pallas_call(
        factor_kernel,
        grid_spec=pltpu.PrefetchScalarGridSpec(
            num_scalar_prefetch=1,
            grid=(2 * KEEP,),
            in_specs=[
                pl.BlockSpec(
                    (groups, 2, 1, rows, FB), lambda k, m: (0, 0, jnp.minimum(k, KEEP - 1), 0, 0)
                )
            ],
            out_specs=[
                pl.BlockSpec((1, FB, FB), lambda k, m: (k, 0, 0)),
                pl.BlockSpec((1, FB, FB), lambda k, m: (k, 0, 0)),
                pl.BlockSpec(
                    (2, 1, FB, FB), lambda k, m: (0, jnp.minimum(k, KEEP - 1), 0, 0)
                ),
            ],
        ),
        out_shape=[out, out, jax.ShapeDtypeStruct((2, KEEP, FB, FB), jnp.bfloat16)],
        compiler_params=pltpu.CompilerParams(vmem_limit_bytes=48 << 20),
        name="factor_gram",
    )(mine, f_in)


def cross_kernel(swap_pairs, mine, l_in, f_in, out, hand):
    k = pl.program_id(0)

    @pl.when(k < KEEP)
    def _():
        keep = mine[0] != 0
        last = l_in[:, 0]
        groups, rows, _ = last.shape
        if swap_pairs:
            pairs = last.reshape(groups // 2, 2, rows, FB)
            turned = jnp.concatenate([pairs[:, 1:], pairs[:, :1]], axis=1).reshape(last.shape)
            last = jnp.where(mine[1] != 0, turned, last)
        r = gram(last.reshape(-1, FB), f_in[:, 0, 0].reshape(-1, FB))
        out[0] = jnp.where(keep, r, 0.0)
        hand[0] = r.astype(jnp.bfloat16)

    @pl.when(k >= KEEP)
    def _():
        out[...] = jnp.zeros_like(out)


def cross(mine, l_in, f_in, which, swap_pairs):
    groups, _, rows, _ = l_in.shape
    return pl.pallas_call(
        functools.partial(cross_kernel, swap_pairs),
        grid_spec=pltpu.PrefetchScalarGridSpec(
            num_scalar_prefetch=1,
            grid=(2 * KEEP,),
            in_specs=[
                pl.BlockSpec((groups, 1, rows, FB), lambda k, m: (0, jnp.minimum(k, KEEP - 1), 0, 0)),
                pl.BlockSpec(
                    (groups, 1, 1, rows, FB),
                    lambda k, m: (0, which, jnp.minimum(k, KEEP - 1), 0, 0),
                ),
            ],
            out_specs=[
                pl.BlockSpec((1, FB, FB), lambda k, m: (k, 0, 0)),
                pl.BlockSpec((1, FB, FB), lambda k, m: (jnp.minimum(k, KEEP - 1), 0, 0)),
            ],
        ),
        out_shape=[
            jax.ShapeDtypeStruct((2 * KEEP, FB, FB), jnp.float32),
            jax.ShapeDtypeStruct((KEEP, FB, FB), jnp.bfloat16),
        ],
        compiler_params=pltpu.CompilerParams(vmem_limit_bytes=48 << 20),
        name="cross_gram",
    )(mine, l_in, f_in)


def fill_kernel(flag, got, old, out, half, wide, sem):
    @pl.when(flag[0] != 0)
    def _():
        load = pltpu.make_async_copy(got, half, sem)
        load.start()
        load.wait()
        wide[...] = half[...].astype(jnp.float32)
        store = pltpu.make_async_copy(wide, out.at[pl.ds(KEEP, KEEP)], sem)
        store.start()
        store.wait()


def fill(flag, got, old):
    return pl.pallas_call(
        fill_kernel,
        in_specs=[
            pl.BlockSpec(memory_space=pltpu.SMEM),
            pl.BlockSpec(memory_space=pl.ANY),
            pl.BlockSpec(memory_space=pl.ANY),
        ],
        out_specs=pl.BlockSpec(memory_space=pl.ANY),
        out_shape=jax.ShapeDtypeStruct(old.shape, old.dtype),
        scratch_shapes=[
            pltpu.VMEM(got.shape, jnp.bfloat16),
            pltpu.VMEM(got.shape, jnp.float32),
            pltpu.SemaphoreType.DMA,
        ],
        input_output_aliases={2: 0},
        name="fill_slots",
    )(flag, got, old)


def hand_over(route, groups, *blocks):
    axes = ("section", "dp")
    sections = lax.axis_size("section")

    def along(spare, full, *values):
        pairs = [(s * groups + spare, s * groups + full) for s in range(sections)]
        return tuple(lax.ppermute(v, axes, pairs) for v in values)

    cases = [(s, f) for s in range(1, groups - 1) for f in range(groups) if f != s]
    return lax.switch(route, [functools.partial(along, s, f) for s, f in cases], *blocks)


def on_device(first_acts, first_grads, last_acts, last_grads, doc_lengths, block_owner):
    row_count = first_acts.shape[1]
    groups = lax.axis_size("dp")
    sections = lax.axis_size("section")
    axes = ("section", "dp")
    me = lax.axis_index("dp")
    section = lax.axis_index("section")
    weight = row_scale(doc_lengths[0], row_count, doc_lengths.shape[1] * groups)[:, None]
    order, spare, full = placement(block_owner, groups)
    route = (spare - 1) * (groups - 1) + full - jnp.where(full > spare, 1, 0)
    boundary = sections // 2
    mine = jnp.stack([me != spare, section == boundary]).astype(jnp.int32)
    receive = (me == full).astype(jnp.int32).reshape(1)

    f, la, lg = scale_and_sort(
        order, weight, first_acts[0], first_grads[0], last_acts[0], last_grads[0], groups
    )
    straight = [(s * groups + d, (s + 1) * groups + d) for s in range(sections - 1) for d in range(groups)]
    turned = [
        (s * groups + d, (s + 1) * groups + (d ^ 1 if s + 1 == boundary else d))
        for s in range(sections - 1)
        for d in range(groups)
    ]
    la = lax.ppermute(la, axes, straight)
    lg = lax.ppermute(lg, axes, turned)

    def exchange(x):
        return lax.all_to_all(x, "dp", split_axis=0, concat_axis=0, tiled=True)

    f_in = exchange(f)
    la_in = exchange(la)
    lg_in = exchange(lg)
    af, gf, f_hand = factors(mine, f_in)
    ac, ac_hand = cross(mine, la_in, f_in, 0, False)
    gc, gc_hand = cross(mine, lg_in, f_in, 1, True)
    (f_got,) = hand_over(route, groups, f_hand)
    (ac_got,) = hand_over(route, groups, ac_hand)
    (gc_got,) = hand_over(route, groups, gc_hand)
    af = fill(receive, f_got[0], af)
    gf = fill(receive, f_got[1], gf)
    ac = fill(receive, ac_got, ac)
    gc = fill(receive, gc_got, gc)
    return af[None, None], gf[None, None], ac[None, None], gc[None, None]


def solution(mesh):
    placed = (
        P("section", "dp", None),
        P("section", "dp", None),
        P("section", "dp", None),
        P("section", "dp", None),
        P("dp", None),
        P(),
    )
    return jax.shard_map(
        on_device,
        mesh=mesh,
        in_specs=placed,
        out_specs=(P("section", "dp", None, None, None),) * 4,
        check_vma=False,
    )
```

```python
import functools

import jax
import jax.numpy as jnp
import numpy as np
from jax import lax
from jax.experimental import pallas as pl
from jax.experimental.pallas import tpu as pltpu
from jax.sharding import PartitionSpec as P

KEEP = 2
QUADS = 7
AXES = ("section", "dp")


def chains(spare, full):
    xs, ys, xf, yf = spare // 2, spare % 2, full // 2, full % 2
    at = lambda x, y: (x % 4) * 2 + y
    step = (xf - xs) % 4
    if step == 0:
        return [], [at(xs + 1, ys), at(xs + 1, yf)]
    if ys != yf:
        return [], [at(xs, yf)]
    if step == 2:
        return [at(xs + 1, ys)], [at(xs - 1, ys)]
    return [], [at(xs, 1 - ys), at(xf, 1 - ys)]


def routes(groups):
    return [(s, f) for s in range(1, groups - 1) for f in range(groups) if f != s]


def plan_table(groups):
    table = np.zeros((groups * groups, 16), np.int32)
    for number, (spare, full) in enumerate(routes(groups)):
        row = table[spare * groups + full]
        row[:groups] = np.arange(groups) * KEEP + 1
        for way, between in enumerate(chains(spare, full)):
            slot = spare * KEEP + way
            for g in between:
                row[g] = slot
                slot = g * KEEP + 1
                row[groups + 2 + way] |= 1 << g
            row[groups + way] = slot
        row[groups + 4] = number
    return table.reshape(-1)


def prepare_kernel(groups, split, lengths, owner, table, one, two, *refs):
    outs, (meta, order, slots, counts) = refs[:-4], refs[-4:]
    blocks = owner.shape[0]
    step = pl.program_id(0)
    me = lax.axis_index("dp")

    @pl.when(step == 0)
    def _():
        for g in range(groups):
            counts[g] = 0
        for b in range(blocks):
            o = owner[b]
            slots[b] = counts[o]
            counts[o] = counts[o] + 1
        spare, full = jnp.int32(0), jnp.int32(0)
        for g in range(groups):
            spare = jnp.where(counts[g] == 0, g, spare)
            full = jnp.where(counts[g] > KEEP, g, full)
        row = (spare * groups + full) * 16
        for b in range(blocks):
            o, k = owner[b], slots[b]
            at = jnp.where(k <= 1, o, groups + jnp.minimum(k, 3) - 2)
            place = jnp.where(k == 0, o * KEEP, table[row + at])
            order[place] = b
        on_a = (table[row + groups + 2] >> me) & 1
        on_b = (table[row + groups + 3] >> me) & 1
        last = (me == full).astype(jnp.int32)
        meta[0] = (me == spare).astype(jnp.int32)
        meta[1] = on_a | on_b
        meta[2] = on_a + 2 * last
        meta[3] = on_b + 3 * last
        meta[4] = table[row + groups + 4]

    rows, width = one.shape
    feat = width // blocks
    row_at = lax.broadcasted_iota(jnp.int32, (rows, feat), 0) + step * rows
    length = jnp.ones((rows, feat), jnp.float32)
    start = jnp.int32(0)
    for d in range(lengths.shape[1]):
        size = lengths[0, d]
        inside = (row_at >= start) & (row_at < start + size)
        length = jnp.where(inside, size.astype(jnp.float32), length)
        start = start + size
    weight = jnp.sqrt((1.0 / length) / (lengths.shape[1] * groups))
    half = me % 2
    for x in range(groups // 2):
        for t in range(2):
            for k in range(KEEP):
                source = order[x * 4 + (half ^ t) * KEEP + k]
                columns = pl.ds(pl.multiple_of(source * feat, feat), feat)
                for a, ref in ((0, one), (1, two)):
                    value = (ref[:, columns].astype(jnp.float32) * weight).astype(jnp.bfloat16)
                    if split:
                        outs[2 * a + t][x, k] = value
                    else:
                        outs[0][x, t, a, k] = value


def prepare(lengths, owner, table, one, two, groups, split):
    rows, width = one.shape
    feat = width // owner.shape[0]
    cut = rows // 4
    wide = groups // 2
    if split:
        shapes = [(wide, KEEP, rows, feat)] * 4
    else:
        shapes = [(wide, 2, 2, KEEP, rows, feat)]
    smem = pl.BlockSpec(memory_space=pltpu.SMEM)
    take = pl.BlockSpec((cut, width), lambda i: (i, 0))

    def give(shape):
        lead = len(shape) - 2
        return pl.BlockSpec(shape[:lead] + (cut, feat), lambda i: (0,) * lead + (i, 0))

    return pl.pallas_call(
        functools.partial(prepare_kernel, groups, split),
        grid=(rows // cut,),
        in_specs=[smem, smem, smem, take, take],
        out_specs=[give(s) for s in shapes] + [smem],
        out_shape=[jax.ShapeDtypeStruct(s, jnp.bfloat16) for s in shapes]
        + [jax.ShapeDtypeStruct((8,), jnp.int32)],
        scratch_shapes=[
            pltpu.SMEM((owner.shape[0],), jnp.int32),
            pltpu.SMEM((owner.shape[0],), jnp.int32),
            pltpu.SMEM((groups,), jnp.int32),
        ],
        compiler_params=pltpu.CompilerParams(vmem_limit_bytes=60 << 20),
        name="prepare",
    )(lengths, owner, table, one, two)


def dot_rows(x, y):
    return lax.dot_general(x, y, (((0,), (0,)), ((), ())), preferred_element_type=jnp.float32)


def pack(ref, factor, between):
    h = factor.shape[0] // 2
    corners = [(0, 0), (0, 1), (1, 1)]
    pieces = [factor[i * h : i * h + h, j * h : j * h + h] for i, j in corners]
    pieces += [between[i * h : i * h + h, j * h : j * h + h] for i in range(2) for j in range(2)]
    for n, piece in enumerate(pieces):
        ref[0, n] = piece.astype(jnp.bfloat16)


def gram_kernel(meta, own, other, last, *refs):
    factor_out, between_out, way_a, way_b = refs[-4:]
    k = pl.program_id(0)

    @pl.when(k < KEEP)
    def _():
        feat = own.shape[-1]
        f0, f1 = own[:, 0, 0, 0].reshape(-1, feat), other[:, 0].reshape(-1, feat)
        l0, l1 = last[:, 0, 0].reshape(-1, feat), last[:, 1, 0].reshape(-1, feat)
        factor = dot_rows(f0, f0) + dot_rows(f1, f1)
        between = dot_rows(l0, f0) + dot_rows(l1, f1)
        spare = meta[0] != 0
        foreign = spare | ((meta[1] != 0) & (k == 1))

        @pl.when(jnp.logical_not(foreign))
        def _():
            factor_out[0] = factor
            between_out[0] = between

        @pl.when(foreign)
        def _():
            factor_out[...] = jnp.zeros_like(factor_out)
            between_out[...] = jnp.zeros_like(between_out)

            @pl.when(spare == (k == 0))
            def _():
                pack(way_a, factor, between)

            @pl.when(k == 1)
            def _():
                pack(way_b, factor, between)

    @pl.when(k >= KEEP)
    def _():
        factor_out[...] = jnp.zeros_like(factor_out)
        between_out[...] = jnp.zeros_like(between_out)


def grams(meta, kind, f_in, f_swap, l_in, ways):
    wide, _, _, _, rows, feat = f_in.shape
    at = lambda k: jnp.minimum(k, KEEP - 1)
    out = jax.ShapeDtypeStruct((2 * KEEP, feat, feat), jnp.float32)
    way = jax.ShapeDtypeStruct((2, QUADS, feat // 2, feat // 2), jnp.bfloat16)
    out_spec = pl.BlockSpec((1, feat, feat), lambda k, m: (k, 0, 0))
    way_spec = pl.BlockSpec((1, QUADS, feat // 2, feat // 2), lambda k, m: (kind, 0, 0, 0))
    return pl.pallas_call(
        gram_kernel,
        grid_spec=pltpu.PrefetchScalarGridSpec(
            num_scalar_prefetch=1,
            grid=(2 * KEEP,),
            in_specs=[
                pl.BlockSpec((wide, 1, 1, 1, rows, feat), lambda k, m: (0, 0, kind, at(k), 0, 0)),
                pl.BlockSpec((wide, 1, rows, feat), lambda k, m: (0, at(k), 0, 0)),
                pl.BlockSpec((wide, 2, 1, rows, feat), lambda k, m: (0, 0, at(k), 0, 0)),
            ]
            + [pl.BlockSpec(memory_space=pl.ANY)] * len(ways),
            out_specs=[out_spec, out_spec, way_spec, way_spec],
        ),
        out_shape=[out, out, way, way],
        input_output_aliases={4 + n: 2 + n for n in range(len(ways))},
        compiler_params=pltpu.CompilerParams(vmem_limit_bytes=48 << 20),
        name="grams",
    )(meta, f_in, f_swap, l_in, *ways)


def fill_kernel(meta, way_a, way_b, *refs):
    outs, (half, wide, sem) = refs[4:8], refs[8:]
    feat = wide.shape[-1]
    h = feat // 2

    def place(way, slot):
        load = pltpu.make_async_copy(way, half, sem)
        load.start()
        load.wait()
        for kind in range(2):
            for n, (i, j) in enumerate([(0, 0), (0, 1), (1, 1)]):
                piece = half[kind, n].astype(jnp.float32)
                wide[2 * kind, i * h : i * h + h, j * h : j * h + h] = piece
                if i != j:
                    wide[2 * kind, j * h : j * h + h, i * h : i * h + h] = piece.T
            for n in range(4):
                i, j = n // 2, n % 2
                piece = half[kind, 3 + n].astype(jnp.float32)
                wide[2 * kind + 1, i * h : i * h + h, j * h : j * h + h] = piece
        stores = [pltpu.make_async_copy(wide.at[n], outs[n].at[slot], sem) for n in range(4)]
        for store in stores:
            store.start()
        for store in stores:
            store.wait()

    @pl.when(meta[2] != 0)
    def _():
        place(way_a, meta[2])

    @pl.when(meta[3] != 0)
    def _():
        place(way_b, meta[3])


def fill(meta, way_a, way_b, outs):
    feat = outs[0].shape[-1]
    anywhere = pl.BlockSpec(memory_space=pl.ANY)
    return pl.pallas_call(
        fill_kernel,
        in_specs=[pl.BlockSpec(memory_space=pltpu.SMEM)] + [anywhere] * 6,
        out_specs=[anywhere] * 4,
        out_shape=[jax.ShapeDtypeStruct(o.shape, o.dtype) for o in outs],
        scratch_shapes=[
            pltpu.VMEM(way_a.shape, jnp.bfloat16),
            pltpu.VMEM((4, feat, feat), jnp.float32),
            pltpu.SemaphoreType.DMA,
        ],
        input_output_aliases={3 + n: n for n in range(4)},
        compiler_params=pltpu.CompilerParams(vmem_limit_bytes=40 << 20),
        name="fill_slots",
    )(meta, way_a, way_b, *outs)


def hand_over(route, groups, way_a, way_b):
    sections = lax.axis_size("section")

    def along(spare, full, *values):
        sent = []
        for value, between in zip(values, chains(spare, full)):
            stops = [spare] + between + [full]
            pairs = [(s * groups + i, s * groups + j) for s in range(sections) for i, j in zip(stops, stops[1:])]
            sent.append(lax.ppermute(value, AXES, pairs))
        return tuple(sent)

    return lax.switch(route, [functools.partial(along, s, f) for s, f in routes(groups)], way_a, way_b)


def on_device(first_acts, first_grads, last_acts, last_grads, doc_lengths, block_owner):
    groups = lax.axis_size("dp")
    sections = lax.axis_size("section")
    table = jnp.asarray(plan_table(groups))
    (f, meta) = prepare(doc_lengths, block_owner, table, first_acts[0], first_grads[0], groups, False)
    meta, last_acts, last_grads = lax.optimization_barrier((meta, last_acts, last_grads))
    *l, _ = prepare(doc_lengths, block_owner, table, last_acts[0], last_grads[0], groups, True)

    straight = [(s * groups + d, (s + 1) * groups + d) for s in range(sections - 1) for d in range(groups)]
    across = [(i, j ^ 1) for i, j in straight]
    swap = [(i, i ^ 1) for i in range(sections * groups)]
    rows_of = [[d for d in range(groups) if d % 2 == y] for y in range(2)]

    def exchange(x):
        return lax.all_to_all(x, "dp", split_axis=0, concat_axis=0, tiled=True, axis_index_groups=rows_of)

    f_in = exchange(f)
    moved = [lax.ppermute(v, AXES, across if n % 2 else straight) for n, v in enumerate(l)]
    moved, f_in = lax.optimization_barrier((moved, f_in))
    outs, ways = [], []
    for kind in range(2):
        f_swap = lax.ppermute(f_in[:, 1, kind], AXES, swap)
        l_in = exchange(jnp.stack(moved[2 * kind : 2 * kind + 2], axis=1))
        moved, f_in, f_swap, l_in = lax.optimization_barrier((moved, f_in, f_swap, l_in))
        factor, between, *ways = grams(meta, kind, f_in, f_swap, l_in, ways)
        outs += [factor, between]
    got = hand_over(meta[4], groups, *ways)
    af, ac, gf, gc = fill(meta, *got, outs)
    return af[None, None], gf[None, None], ac[None, None], gc[None, None]


def solution(mesh):
    placed = (
        P("section", "dp", None),
        P("section", "dp", None),
        P("section", "dp", None),
        P("section", "dp", None),
        P("dp", None),
        P(),
    )
    return jax.shard_map(
        on_device,
        mesh=mesh,
        in_specs=placed,
        out_specs=(P("section", "dp", None, None, None),) * 4,
        check_vma=False,
    )
```

```python
import functools

import jax
import jax.numpy as jnp
import numpy as np
from jax import lax
from jax.experimental import pallas as pl
from jax.experimental.pallas import tpu as pltpu
from jax.sharding import PartitionSpec as P

KEEP = 2
AXES = ("section", "dp")


def chains(spare, full):
    xs, ys, xf, yf = spare // 2, spare % 2, full // 2, full % 2
    at = lambda x, y: (x % 4) * 2 + y
    step = (xf - xs) % 4
    if step == 0:
        return [], [at(xs + 1, ys), at(xs + 1, yf)]
    if ys != yf:
        return [], [at(xs, yf)]
    if step == 2:
        return [at(xs + 1, ys)], [at(xs - 1, ys)]
    return [], [at(xs, 1 - ys), at(xf, 1 - ys)]


def routes(groups):
    return [(s, f) for s in range(1, groups - 1) for f in range(groups) if f != s]


def plan_table(groups):
    table = np.zeros((groups * groups, 16), np.int32)
    for number, (spare, full) in enumerate(routes(groups)):
        row = table[spare * groups + full]
        row[:groups] = np.arange(groups) * KEEP + 1
        for way, between in enumerate(chains(spare, full)):
            slot = spare * KEEP + way
            for g in between:
                row[g] = slot
                slot = g * KEEP + 1
                row[groups + 2 + way] |= 1 << g
            row[groups + way] = slot
        row[groups + 4] = number
    return table.reshape(-1)


def prepare_kernel(groups, split, lengths, owner, table, one, two, *refs):
    outs, (meta, order, slots, counts) = refs[:-4], refs[-4:]
    blocks = owner.shape[0]
    step = pl.program_id(0)
    me = lax.axis_index("dp")

    @pl.when(step == 0)
    def _():
        for g in range(groups):
            counts[g] = 0
        for b in range(blocks):
            o = owner[b]
            slots[b] = counts[o]
            counts[o] = counts[o] + 1
        spare, full = jnp.int32(0), jnp.int32(0)
        for g in range(groups):
            spare = jnp.where(counts[g] == 0, g, spare)
            full = jnp.where(counts[g] > KEEP, g, full)
        row = (spare * groups + full) * 16
        for b in range(blocks):
            o, k = owner[b], slots[b]
            at = jnp.where(k <= 1, o, groups + jnp.minimum(k, 3) - 2)
            place = jnp.where(k == 0, o * KEEP, table[row + at])
            order[place] = b
        on_a = (table[row + groups + 2] >> me) & 1
        on_b = (table[row + groups + 3] >> me) & 1
        last = (me == full).astype(jnp.int32)
        meta[0] = (me == spare).astype(jnp.int32)
        meta[1] = on_a | on_b
        meta[2] = on_a + 2 * last
        meta[3] = on_b + 3 * last
        meta[4] = table[row + groups + 4]

    rows, width = one.shape
    feat = width // blocks
    row_at = lax.broadcasted_iota(jnp.int32, (rows, feat), 0) + step * rows
    length = jnp.ones((rows, feat), jnp.float32)
    start = jnp.int32(0)
    for d in range(lengths.shape[1]):
        size = lengths[0, d]
        inside = (row_at >= start) & (row_at < start + size)
        length = jnp.where(inside, size.astype(jnp.float32), length)
        start = start + size
    weight = jnp.sqrt((1.0 / length) / (lengths.shape[1] * groups))
    half = me % 2
    for x in range(groups // 2):
        for t in range(2):
            for k in range(KEEP):
                source = order[x * 4 + (half ^ t) * KEEP + k]
                columns = pl.ds(pl.multiple_of(source * feat, feat), feat)
                for a, ref in ((0, one), (1, two)):
                    value = (ref[:, columns].astype(jnp.float32) * weight).astype(jnp.bfloat16)
                    if split:
                        outs[t][x, a, k] = value
                    else:
                        outs[0][x, t, a, k] = value


def prepare(lengths, owner, table, one, two, groups, split):
    rows, width = one.shape
    feat = width // owner.shape[0]
    cut = rows // 4
    wide = groups // 2
    if split:
        shapes = [(wide, 2, KEEP, rows, feat)] * 2
    else:
        shapes = [(wide, 2, 2, KEEP, rows, feat)]
    smem = pl.BlockSpec(memory_space=pltpu.SMEM)
    take = pl.BlockSpec((cut, width), lambda i: (i, 0))

    def give(shape):
        lead = len(shape) - 2
        return pl.BlockSpec(shape[:lead] + (cut, feat), lambda i: (0,) * lead + (i, 0))

    return pl.pallas_call(
        functools.partial(prepare_kernel, groups, split),
        grid=(rows // cut,),
        in_specs=[smem, smem, smem, take, take],
        out_specs=[give(s) for s in shapes] + [smem],
        out_shape=[jax.ShapeDtypeStruct(s, jnp.bfloat16) for s in shapes]
        + [jax.ShapeDtypeStruct((8,), jnp.int32)],
        scratch_shapes=[
            pltpu.SMEM((owner.shape[0],), jnp.int32),
            pltpu.SMEM((owner.shape[0],), jnp.int32),
            pltpu.SMEM((groups,), jnp.int32),
        ],
        compiler_params=pltpu.CompilerParams(vmem_limit_bytes=60 << 20),
        name="prepare",
    )(lengths, owner, table, one, two)


def dot_rows(x, y):
    return lax.dot_general(x, y, (((0,), (0,)), ((), ())), preferred_element_type=jnp.float32)


def corners(matrix, symmetric):
    h = matrix.shape[0] // 2
    return [
        matrix[i * h : i * h + h, j * h : j * h + h].astype(jnp.bfloat16)
        for i in range(2)
        for j in range(2)
        if i <= j or not symmetric
    ]


def begin_kernel(own, last, *outs):
    k = pl.program_id(0)

    @pl.when(k < KEEP)
    def _():
        feat = own.shape[-1]
        for kind in range(2):
            f = own[:, 0, kind, 0].reshape(-1, feat)
            l = last[:, kind, 0].reshape(-1, feat)
            outs[2 * kind][0] = dot_rows(f, f)
            outs[2 * kind + 1][0] = dot_rows(l, f)

    @pl.when(k >= KEEP)
    def _():
        for out in outs:
            out[...] = jnp.zeros_like(out)


def begin(f_in, l_in):
    wide, _, _, _, rows, feat = f_in.shape
    at = lambda k: jnp.minimum(k, KEEP - 1)
    return pl.pallas_call(
        begin_kernel,
        grid=(2 * KEEP,),
        in_specs=[
            pl.BlockSpec((wide, 1, 2, 1, rows, feat), lambda k: (0, 0, 0, at(k), 0, 0)),
            pl.BlockSpec((wide, 2, 1, rows, feat), lambda k: (0, 0, at(k), 0, 0)),
        ],
        out_specs=[pl.BlockSpec((1, feat, feat), lambda k: (k, 0, 0))] * 4,
        out_shape=[jax.ShapeDtypeStruct((2 * KEEP, feat, feat), jnp.float32)] * 4,
        compiler_params=pltpu.CompilerParams(vmem_limit_bytes=60 << 20),
        name="begin",
    )(f_in, l_in)


def finish_kernel(symmetric, base, meta, *refs):
    ins, sums, ways = refs[: 1 if symmetric else 2], refs[-8:-6], refs[-4:-2]
    outs, (packed, sem) = refs[-6:-4], refs[-2:]
    k = pl.program_id(0)
    feat = ins[0].shape[-1]
    spare = meta[0] != 0
    foreign = spare | ((meta[1] != 0) & (k == 1))
    each = 3 if symmetric else 4
    for kind in range(2):
        f = ins[-1][:, kind, 0].reshape(-1, feat)
        l = ins[0][:, kind, 0].reshape(-1, feat)
        total = sums[kind][0] + dot_rows(l, f)
        outs[kind][0] = jnp.where(foreign, 0.0, total)

        @pl.when(foreign)
        def _():
            pieces = corners(total, symmetric)
            for way, chosen in ((0, spare == (k == 0)), (1, k == 1)):

                @pl.when(chosen)
                def _():
                    for n, piece in enumerate(pieces):
                        packed[way, each * kind + n] = piece

    @pl.when(foreign & (k == 1))
    def _():
        copies = [
            pltpu.make_async_copy(packed.at[way], ways[way].at[pl.ds(base, 2 * each)], sem.at[way])
            for way in range(2)
        ]
        for copy in copies:
            copy.start()
        for copy in copies:
            copy.wait()


def finish(meta, f_swap, l_in, sums, ways):
    symmetric = l_in is None
    ins = [f_swap] if symmetric else [l_in, f_swap]
    wide, _, _, rows, feat = f_swap.shape
    each, base = (3, 0) if symmetric else (4, 6)
    way = jax.ShapeDtypeStruct((14, feat // 2, feat // 2), jnp.bfloat16)
    out = jax.ShapeDtypeStruct((2 * KEEP, feat, feat), jnp.float32)
    block = pl.BlockSpec((1, feat, feat), lambda k, m: (k, 0, 0))
    anywhere = pl.BlockSpec(memory_space=pl.ANY)
    aliases = {1 + len(ins) + len(ways) + n: n for n in range(2)}
    aliases.update({1 + len(ins) + n: 2 + n for n in range(len(ways))})
    return pl.pallas_call(
        functools.partial(finish_kernel, symmetric, base),
        grid_spec=pltpu.PrefetchScalarGridSpec(
            num_scalar_prefetch=1,
            grid=(KEEP,),
            in_specs=[pl.BlockSpec((wide, 2, 1, rows, feat), lambda k, m: (0, 0, k, 0, 0))] * len(ins)
            + [anywhere] * len(ways)
            + [block] * 2,
            out_specs=[block] * 2 + [anywhere] * 2,
            scratch_shapes=[
                pltpu.VMEM((2, 2 * each, feat // 2, feat // 2), jnp.bfloat16),
                pltpu.SemaphoreType.DMA((2,)),
            ],
        ),
        out_shape=[out, out, way, way],
        input_output_aliases=aliases,
        compiler_params=pltpu.CompilerParams(vmem_limit_bytes=60 << 20),
        name="finish",
    )(meta, *ins, *ways, *sums)


def fill_kernel(meta, *refs):
    ways, outs, (half, wide, load_sem, store_sem) = refs[:2], refs[6:10], refs[10:]
    feat = wide.shape[-1]
    h = feat // 2
    slots = [meta[2], meta[3]]
    loads = [pltpu.make_async_copy(ways[w], half.at[w], load_sem.at[w]) for w in range(2)]

    def stores(w):
        return [
            pltpu.make_async_copy(wide.at[w, n], outs[n].at[slots[w]], store_sem.at[w, n]) for n in range(4)
        ]

    for w in range(2):

        @pl.when(slots[w] != 0)
        def _():
            loads[w].start()

    for w in range(2):

        @pl.when(slots[w] != 0)
        def _():
            loads[w].wait()
            started = stores(w)
            for kind in range(2):
                for n, (i, j) in enumerate([(0, 0), (0, 1), (1, 1)]):
                    piece = half[w, 3 * kind + n].astype(jnp.float32)
                    wide[w, 2 * kind, i * h : i * h + h, j * h : j * h + h] = piece
                    if i != j:
                        wide[w, 2 * kind, j * h : j * h + h, i * h : i * h + h] = piece.T
                started[2 * kind].start()
                for n in range(4):
                    i, j = n // 2, n % 2
                    piece = half[w, 6 + 4 * kind + n].astype(jnp.float32)
                    wide[w, 2 * kind + 1, i * h : i * h + h, j * h : j * h + h] = piece
                started[2 * kind + 1].start()

    for w in range(2):

        @pl.when(slots[w] != 0)
        def _():
            for store in stores(w):
                store.wait()


def fill(meta, way_a, way_b, outs):
    feat = outs[0].shape[-1]
    anywhere = pl.BlockSpec(memory_space=pl.ANY)
    return pl.pallas_call(
        fill_kernel,
        in_specs=[pl.BlockSpec(memory_space=pltpu.SMEM)] + [anywhere] * 6,
        out_specs=[anywhere] * 4,
        out_shape=[jax.ShapeDtypeStruct(o.shape, o.dtype) for o in outs],
        scratch_shapes=[
            pltpu.VMEM((2,) + way_a.shape, jnp.bfloat16),
            pltpu.VMEM((2, 4, feat, feat), jnp.float32),
            pltpu.SemaphoreType.DMA((2,)),
            pltpu.SemaphoreType.DMA((2, 4)),
        ],
        input_output_aliases={3 + n: n for n in range(4)},
        compiler_params=pltpu.CompilerParams(vmem_limit_bytes=60 << 20),
        name="fill_slots",
    )(meta, way_a, way_b, *outs)


def hand_over(route, groups, way_a, way_b):
    sections = lax.axis_size("section")

    def along(spare, full, *values):
        sent = []
        for value, between in zip(values, chains(spare, full)):
            stops = [spare] + between + [full]
            pairs = [(s * groups + i, s * groups + j) for s in range(sections) for i, j in zip(stops, stops[1:])]
            sent.append(lax.ppermute(value, AXES, pairs))
        return tuple(sent)

    return lax.switch(route, [functools.partial(along, s, f) for s, f in routes(groups)], way_a, way_b)


def on_device(first_acts, first_grads, last_acts, last_grads, doc_lengths, block_owner):
    groups = lax.axis_size("dp")
    sections = lax.axis_size("section")
    table = jnp.asarray(plan_table(groups))
    f, meta = prepare(doc_lengths, block_owner, table, first_acts[0], first_grads[0], groups, False)
    meta, last_acts, last_grads = lax.optimization_barrier((meta, last_acts, last_grads))
    l_own, l_other, _ = prepare(doc_lengths, block_owner, table, last_acts[0], last_grads[0], groups, True)

    straight = [(s * groups + d, (s + 1) * groups + d) for s in range(sections - 1) for d in range(groups)]
    across = [(i, j ^ 1) for i, j in straight]
    swap = [(i, i ^ 1) for i in range(sections * groups)]
    rows_of = [[d for d in range(groups) if d % 2 == y] for y in range(2)]

    def exchange(x):
        return lax.all_to_all(x, "dp", split_axis=0, concat_axis=0, tiled=True, axis_index_groups=rows_of)

    l_own = lax.ppermute(l_own, AXES, straight)
    l_other = lax.ppermute(l_other, AXES, across)
    f_in = exchange(f)
    f_in, l_own = lax.optimization_barrier((f_in, l_own))
    f_swap = lax.ppermute(f_in[:, 1], AXES, swap)
    l_own = exchange(l_own)
    l_own, l_other = lax.optimization_barrier((l_own, l_other))
    l_other = exchange(l_other)
    af, ac, gf, gc = begin(f_in, l_own)
    af, gf, *ways = finish(meta, f_swap, None, (af, gf), ())
    ac, gc, *ways = finish(meta, f_swap, l_other, (ac, gc), ways)
    got = hand_over(meta[4], groups, *ways)
    af, ac, gf, gc = fill(meta, *got, (af, ac, gf, gc))
    return af[None, None], gf[None, None], ac[None, None], gc[None, None]


def solution(mesh):
    placed = (
        P("section", "dp", None),
        P("section", "dp", None),
        P("section", "dp", None),
        P("section", "dp", None),
        P("dp", None),
        P(),
    )
    return jax.shard_map(
        on_device,
        mesh=mesh,
        in_specs=placed,
        out_specs=(P("section", "dp", None, None, None),) * 4,
        check_vma=False,
    )
```

```python
import functools

import jax
import jax.numpy as jnp
import numpy as np
from jax import lax
from jax.experimental import pallas as pl
from jax.experimental.pallas import tpu as pltpu
from jax.sharding import PartitionSpec as P

KEEP = 2
AXES = ("section", "dp")


def at(x, y):
    return (x % 4) * 2 + y


def patterns(route):
    if route == 0:
        return [{at(x, y): at(x + step, y) for x in range(4) for y in range(2)} for step in (1, -1)]
    xf, yf = (route - 1) // 2, (route - 1) % 2
    near = 1 - yf
    plus = {at(x, near): at(x + 1, near) for x in range(4)}
    plus[at(xf, near)] = at(xf, yf)
    minus = {at(x, near): at(x - 1, near) for x in range(4)}
    minus[at(xf + 1, near)] = at(xf + 1, yf)
    minus[at(xf + 1, yf)] = at(xf, yf)
    return [plus, minus]


def chains(spare, full):
    ways = []
    for step in patterns(0 if spare % 2 == full % 2 else 1 + full):
        between = [step[spare]]
        while between[-1] != full:
            between.append(step[between[-1]])
        ways.append(between[:-1])
    return ways


def plan_table(groups):
    table = np.zeros((groups * groups, 16), np.int32)
    for spare, full in [(s, f) for s in range(1, groups - 1) for f in range(groups) if f != s]:
        row = table[spare * groups + full]
        row[:groups] = np.arange(groups) * KEEP + 1
        for way, between in enumerate(chains(spare, full)):
            slot = spare * KEEP + way
            for g in between:
                row[g] = slot
                slot = g * KEEP + 1
                row[groups + 2 + way] |= 1 << g
            row[groups + way] = slot
        row[groups + 4] = 0 if spare % 2 == full % 2 else 1 + full
    return table.reshape(-1)


def prepare_kernel(groups, split, lengths, owner, table, one, two, *refs):
    outs, (meta, order, slots, counts) = refs[:-4], refs[-4:]
    blocks = owner.shape[0]
    step = pl.program_id(0)
    me = lax.axis_index("dp")

    @pl.when(step == 0)
    def _():
        for g in range(groups):
            counts[g] = 0
        for b in range(blocks):
            o = owner[b]
            slots[b] = counts[o]
            counts[o] = counts[o] + 1
        spare, full = jnp.int32(0), jnp.int32(0)
        for g in range(groups):
            spare = jnp.where(counts[g] == 0, g, spare)
            full = jnp.where(counts[g] > KEEP, g, full)
        row = (spare * groups + full) * 16
        for b in range(blocks):
            o, k = owner[b], slots[b]
            at = jnp.where(k <= 1, o, groups + jnp.minimum(k, 3) - 2)
            place = jnp.where(k == 0, o * KEEP, table[row + at])
            order[place] = b
        on_a = (table[row + groups + 2] >> me) & 1
        on_b = (table[row + groups + 3] >> me) & 1
        last = (me == full).astype(jnp.int32)
        meta[0] = (me == spare).astype(jnp.int32)
        meta[1] = on_a | on_b
        meta[2] = on_a + 2 * last
        meta[3] = on_b + 3 * last
        meta[4] = table[row + groups + 4]

    rows, width = one.shape
    feat = width // blocks
    row_at = lax.broadcasted_iota(jnp.int32, (rows, feat), 0) + step * rows
    length = jnp.ones((rows, feat), jnp.float32)
    start = jnp.int32(0)
    for d in range(lengths.shape[1]):
        size = lengths[0, d]
        inside = (row_at >= start) & (row_at < start + size)
        length = jnp.where(inside, size.astype(jnp.float32), length)
        start = start + size
    weight = jnp.sqrt((1.0 / length) / (lengths.shape[1] * groups))
    half = me % 2
    for x in range(groups // 2):
        for t in range(2):
            for k in range(KEEP):
                source = order[x * 4 + (half ^ t) * KEEP + k]
                columns = pl.ds(pl.multiple_of(source * feat, feat), feat)
                for a, ref in ((0, one), (1, two)):
                    value = (ref[:, columns].astype(jnp.float32) * weight).astype(jnp.bfloat16)
                    if split:
                        outs[t][x, a, k] = value
                    else:
                        outs[0][x, t, a, k] = value


def prepare(lengths, owner, table, one, two, groups, split):
    rows, width = one.shape
    feat = width // owner.shape[0]
    cut = rows // 4
    wide = groups // 2
    if split:
        shapes = [(wide, 2, KEEP, rows, feat)] * 2
    else:
        shapes = [(wide, 2, 2, KEEP, rows, feat)]
    smem = pl.BlockSpec(memory_space=pltpu.SMEM)
    take = pl.BlockSpec((cut, width), lambda i: (i, 0))

    def give(shape):
        lead = len(shape) - 2
        return pl.BlockSpec(shape[:lead] + (cut, feat), lambda i: (0,) * lead + (i, 0))

    return pl.pallas_call(
        functools.partial(prepare_kernel, groups, split),
        grid=(rows // cut,),
        in_specs=[smem, smem, smem, take, take],
        out_specs=[give(s) for s in shapes] + [smem],
        out_shape=[jax.ShapeDtypeStruct(s, jnp.bfloat16) for s in shapes]
        + [jax.ShapeDtypeStruct((8,), jnp.int32)],
        scratch_shapes=[
            pltpu.SMEM((owner.shape[0],), jnp.int32),
            pltpu.SMEM((owner.shape[0],), jnp.int32),
            pltpu.SMEM((groups,), jnp.int32),
        ],
        compiler_params=pltpu.CompilerParams(vmem_limit_bytes=60 << 20),
        name="prepare",
    )(lengths, owner, table, one, two)


def dot_rows(x, y):
    return lax.dot_general(x, y, (((0,), (0,)), ((), ())), preferred_element_type=jnp.float32)


def corners(matrix, symmetric):
    h = matrix.shape[0] // 2
    return [
        matrix[i * h : i * h + h, j * h : j * h + h].astype(jnp.bfloat16)
        for i in range(2)
        for j in range(2)
        if i <= j or not symmetric
    ]


def begin_kernel(own, last, *outs):
    k = pl.program_id(0)

    @pl.when(k < KEEP)
    def _():
        feat = own.shape[-1]
        for kind in range(2):
            f = own[:, 0, kind, 0].reshape(-1, feat)
            l = last[:, kind, 0].reshape(-1, feat)
            outs[2 * kind][0] = dot_rows(f, f)
            outs[2 * kind + 1][0] = dot_rows(l, f)

    @pl.when(k >= KEEP)
    def _():
        for out in outs:
            out[...] = jnp.zeros_like(out)


def begin(f_in, l_in):
    wide, _, _, _, rows, feat = f_in.shape
    at = lambda k: jnp.minimum(k, KEEP - 1)
    return pl.pallas_call(
        begin_kernel,
        grid=(2 * KEEP,),
        in_specs=[
            pl.BlockSpec((wide, 1, 2, 1, rows, feat), lambda k: (0, 0, 0, at(k), 0, 0)),
            pl.BlockSpec((wide, 2, 1, rows, feat), lambda k: (0, 0, at(k), 0, 0)),
        ],
        out_specs=[pl.BlockSpec((1, feat, feat), lambda k: (k, 0, 0))] * 4,
        out_shape=[jax.ShapeDtypeStruct((2 * KEEP, feat, feat), jnp.float32)] * 4,
        compiler_params=pltpu.CompilerParams(vmem_limit_bytes=60 << 20),
        name="begin",
    )(f_in, l_in)


def finish_kernel(symmetric, base, meta, *refs):
    ins, sums, ways = refs[: 1 if symmetric else 2], refs[-8:-6], refs[-4:-2]
    outs, (packed, sem) = refs[-6:-4], refs[-2:]
    k = pl.program_id(0)
    feat = ins[0].shape[-1]
    spare = meta[0] != 0
    foreign = spare | ((meta[1] != 0) & (k == 1))
    each = 3 if symmetric else 4
    for kind in range(2):
        f = ins[-1][:, kind, 0].reshape(-1, feat)
        l = ins[0][:, kind, 0].reshape(-1, feat)
        total = sums[kind][0] + dot_rows(l, f)
        outs[kind][0] = jnp.where(foreign, 0.0, total)

        @pl.when(foreign)
        def _():
            pieces = corners(total, symmetric)
            for way, chosen in ((0, spare == (k == 0)), (1, k == 1)):

                @pl.when(chosen)
                def _():
                    for n, piece in enumerate(pieces):
                        packed[way, each * kind + n] = piece

    @pl.when(foreign & (k == 1))
    def _():
        copies = [
            pltpu.make_async_copy(packed.at[way], ways[way].at[pl.ds(base, 2 * each)], sem.at[way])
            for way in range(2)
        ]
        for copy in copies:
            copy.start()
        for copy in copies:
            copy.wait()


def finish(meta, f_swap, l_in, sums, ways):
    symmetric = l_in is None
    ins = [f_swap] if symmetric else [l_in, f_swap]
    wide, _, _, rows, feat = f_swap.shape
    each, base = (3, 0) if symmetric else (4, 6)
    way = jax.ShapeDtypeStruct((14, feat // 2, feat // 2), jnp.bfloat16)
    out = jax.ShapeDtypeStruct((2 * KEEP, feat, feat), jnp.float32)
    block = pl.BlockSpec((1, feat, feat), lambda k, m: (k, 0, 0))
    anywhere = pl.BlockSpec(memory_space=pl.ANY)
    aliases = {1 + len(ins) + len(ways) + n: n for n in range(2)}
    aliases.update({1 + len(ins) + n: 2 + n for n in range(len(ways))})
    return pl.pallas_call(
        functools.partial(finish_kernel, symmetric, base),
        grid_spec=pltpu.PrefetchScalarGridSpec(
            num_scalar_prefetch=1,
            grid=(KEEP,),
            in_specs=[pl.BlockSpec((wide, 2, 1, rows, feat), lambda k, m: (0, 0, k, 0, 0))] * len(ins)
            + [anywhere] * len(ways)
            + [block] * 2,
            out_specs=[block] * 2 + [anywhere] * 2,
            scratch_shapes=[
                pltpu.VMEM((2, 2 * each, feat // 2, feat // 2), jnp.bfloat16),
                pltpu.SemaphoreType.DMA((2,)),
            ],
        ),
        out_shape=[out, out, way, way],
        input_output_aliases=aliases,
        compiler_params=pltpu.CompilerParams(vmem_limit_bytes=60 << 20),
        name="finish",
    )(meta, *ins, *ways, *sums)


def fill_kernel(meta, *refs):
    ways, outs, (half, wide, load_sem, store_sem) = refs[:2], refs[6:10], refs[10:]
    feat = wide.shape[-1]
    h = feat // 2
    slots = [meta[2], meta[3]]
    loads = [pltpu.make_async_copy(ways[w], half.at[w], load_sem.at[w]) for w in range(2)]

    def stores(w):
        return [
            pltpu.make_async_copy(wide.at[w, n], outs[n].at[slots[w]], store_sem.at[w, n]) for n in range(4)
        ]

    for w in range(2):

        @pl.when(slots[w] != 0)
        def _():
            loads[w].start()

    for w in range(2):

        @pl.when(slots[w] != 0)
        def _():
            loads[w].wait()
            started = stores(w)
            for kind in range(2):
                for n, (i, j) in enumerate([(0, 0), (0, 1), (1, 1)]):
                    piece = half[w, 3 * kind + n].astype(jnp.float32)
                    wide[w, 2 * kind, i * h : i * h + h, j * h : j * h + h] = piece
                    if i != j:
                        wide[w, 2 * kind, j * h : j * h + h, i * h : i * h + h] = piece.T
                started[2 * kind].start()
                for n in range(4):
                    i, j = n // 2, n % 2
                    piece = half[w, 6 + 4 * kind + n].astype(jnp.float32)
                    wide[w, 2 * kind + 1, i * h : i * h + h, j * h : j * h + h] = piece
                started[2 * kind + 1].start()

    for w in range(2):

        @pl.when(slots[w] != 0)
        def _():
            for store in stores(w):
                store.wait()


def fill(meta, way_a, way_b, outs):
    feat = outs[0].shape[-1]
    anywhere = pl.BlockSpec(memory_space=pl.ANY)
    return pl.pallas_call(
        fill_kernel,
        in_specs=[pl.BlockSpec(memory_space=pltpu.SMEM)] + [anywhere] * 6,
        out_specs=[anywhere] * 4,
        out_shape=[jax.ShapeDtypeStruct(o.shape, o.dtype) for o in outs],
        scratch_shapes=[
            pltpu.VMEM((2,) + way_a.shape, jnp.bfloat16),
            pltpu.VMEM((2, 4, feat, feat), jnp.float32),
            pltpu.SemaphoreType.DMA((2,)),
            pltpu.SemaphoreType.DMA((2, 4)),
        ],
        input_output_aliases={3 + n: n for n in range(4)},
        compiler_params=pltpu.CompilerParams(vmem_limit_bytes=60 << 20),
        name="fill_slots",
    )(meta, way_a, way_b, *outs)


def hand_over(route, groups, way_a, way_b):
    sections = lax.axis_size("section")

    def along(number, *values):
        sent = []
        for value, step in zip(values, patterns(number)):
            pairs = [(s * groups + i, s * groups + j) for s in range(sections) for i, j in step.items()]
            sent.append(lax.ppermute(value, AXES, pairs))
        return tuple(sent)

    return lax.switch(route, [functools.partial(along, n) for n in range(groups + 1)], way_a, way_b)


def on_device(first_acts, first_grads, last_acts, last_grads, doc_lengths, block_owner):
    groups = lax.axis_size("dp")
    sections = lax.axis_size("section")
    table = jnp.asarray(plan_table(groups))
    f, meta = prepare(doc_lengths, block_owner, table, first_acts[0], first_grads[0], groups, False)
    meta, last_acts, last_grads = lax.optimization_barrier((meta, last_acts, last_grads))
    l_own, l_other, _ = prepare(doc_lengths, block_owner, table, last_acts[0], last_grads[0], groups, True)

    straight = [(s * groups + d, (s + 1) * groups + d) for s in range(sections - 1) for d in range(groups)]
    across = [(i, j ^ 1) for i, j in straight]
    swap = [(i, i ^ 1) for i in range(sections * groups)]
    rows_of = [[d for d in range(groups) if d % 2 == y] for y in range(2)]

    def exchange(x):
        return lax.all_to_all(x, "dp", split_axis=0, concat_axis=0, tiled=True, axis_index_groups=rows_of)

    l_own = lax.ppermute(l_own, AXES, straight)
    l_other = lax.ppermute(l_other, AXES, across)
    f_in = exchange(f)
    f_in, l_own = lax.optimization_barrier((f_in, l_own))
    f_swap = lax.ppermute(f_in[:, 1], AXES, swap)
    l_own = exchange(l_own)
    l_own, l_other = lax.optimization_barrier((l_own, l_other))
    l_other = exchange(l_other)
    af, ac, gf, gc = begin(f_in, l_own)
    af, gf, *ways = finish(meta, f_swap, None, (af, gf), ())
    ac, gc, *ways = finish(meta, f_swap, l_other, (ac, gc), ways)
    got = hand_over(meta[4], groups, *ways)
    af, ac, gf, gc = fill(meta, *got, (af, ac, gf, gc))
    return af[None, None], gf[None, None], ac[None, None], gc[None, None]


def solution(mesh):
    placed = (
        P("section", "dp", None),
        P("section", "dp", None),
        P("section", "dp", None),
        P("section", "dp", None),
        P("dp", None),
        P(),
    )
    return jax.shard_map(
        on_device,
        mesh=mesh,
        in_specs=placed,
        out_specs=(P("section", "dp", None, None, None),) * 4,
        check_vma=False,
    )
```

```python
import functools

import jax
import jax.numpy as jnp
import numpy as np
from jax import lax
from jax.experimental import pallas as pl
from jax.experimental.pallas import tpu as pltpu
from jax.sharding import PartitionSpec as P

KEEP = 2
AXES = ("section", "dp")


def at(x, y):
    return (x % 4) * 2 + y


def patterns(route):
    if route == 0:
        return [{at(x, y): at(x + step, y) for x in range(4) for y in range(2)} for step in (1, -1)]
    xf, yf = (route - 1) // 2, (route - 1) % 2
    near = 1 - yf
    plus = {at(x, near): at(x + 1, near) for x in range(4)}
    plus[at(xf, near)] = at(xf, yf)
    minus = {at(x, near): at(x - 1, near) for x in range(4)}
    minus[at(xf + 1, near)] = at(xf + 1, yf)
    minus[at(xf + 1, yf)] = at(xf, yf)
    return [plus, minus]


def chains(spare, full):
    ways = []
    for step in patterns(0 if spare % 2 == full % 2 else 1 + full):
        between = [step[spare]]
        while between[-1] != full:
            between.append(step[between[-1]])
        ways.append(between[:-1])
    return ways


def plan_table(groups):
    table = np.zeros((groups * groups, 16), np.int32)
    for spare, full in [(s, f) for s in range(1, groups - 1) for f in range(groups) if f != s]:
        row = table[spare * groups + full]
        row[:groups] = np.arange(groups) * KEEP + 1
        for way, between in enumerate(chains(spare, full)):
            slot = spare * KEEP + way
            for g in between:
                row[g] = slot
                slot = g * KEEP + 1
                row[groups + 2 + way] |= 1 << g
            row[groups + way] = slot
        row[groups + 4] = 0 if spare % 2 == full % 2 else 1 + full
    return table.reshape(-1)


def prepare_kernel(groups, relative, lengths, owner, table, one, two, *refs):
    outs, (meta, order, slots, counts) = refs[:-4], refs[-4:]
    blocks = owner.shape[0]
    step = pl.program_id(0)
    me = lax.axis_index("dp")

    @pl.when(step == 0)
    def _():
        for g in range(groups):
            counts[g] = 0
        for b in range(blocks):
            o = owner[b]
            slots[b] = counts[o]
            counts[o] = counts[o] + 1
        spare, full = jnp.int32(0), jnp.int32(0)
        for g in range(groups):
            spare = jnp.where(counts[g] == 0, g, spare)
            full = jnp.where(counts[g] > KEEP, g, full)
        row = (spare * groups + full) * 16
        for b in range(blocks):
            o, k = owner[b], slots[b]
            at = jnp.where(k <= 1, o, groups + jnp.minimum(k, 3) - 2)
            place = jnp.where(k == 0, o * KEEP, table[row + at])
            order[place] = b
        on_a = (table[row + groups + 2] >> me) & 1
        on_b = (table[row + groups + 3] >> me) & 1
        last = (me == full).astype(jnp.int32)
        meta[0] = (me == spare).astype(jnp.int32)
        meta[1] = on_a | on_b
        meta[2] = on_a + 2 * last
        meta[3] = on_b + 3 * last
        meta[4] = table[row + groups + 4]

    rows, width = one.shape
    feat = width // blocks
    lanes = 128
    row_at = lax.broadcasted_iota(jnp.int32, (rows, lanes), 0) + step * rows
    length = jnp.ones((rows, lanes), jnp.float32)
    start = jnp.int32(0)
    for d in range(lengths.shape[1]):
        size = lengths[0, d]
        inside = (row_at >= start) & (row_at < start + size)
        length = jnp.where(inside, size.astype(jnp.float32), length)
        start = start + size
    weight = jnp.sqrt((1.0 / length) / (lengths.shape[1] * groups))
    weight = jnp.concatenate([weight] * (feat // lanes), axis=1)
    half = me % 2
    for x in range(groups // 2):
        for t in range(2):
            for k in range(KEEP):
                column = (me // 2 + x) % 4 if relative else x
                source = order[column * 4 + (half ^ t) * KEEP + k]
                columns = pl.ds(pl.multiple_of(source * feat, feat), feat)
                for a, ref in ((0, one), (1, two)):
                    value = (ref[:, columns].astype(jnp.float32) * weight).astype(jnp.bfloat16)
                    outs[t][x, a, k] = value


def prepare(lengths, owner, table, one, two, groups, relative):
    rows, width = one.shape
    feat = width // owner.shape[0]
    cut = rows // 4
    wide = groups // 2
    shapes = [(wide, 2, KEEP, rows, feat)] * 2
    smem = pl.BlockSpec(memory_space=pltpu.SMEM)
    take = pl.BlockSpec((cut, width), lambda i: (i, 0))

    def give(shape):
        lead = len(shape) - 2
        return pl.BlockSpec(shape[:lead] + (cut, feat), lambda i: (0,) * lead + (i, 0))

    return pl.pallas_call(
        functools.partial(prepare_kernel, groups, relative),
        grid=(rows // cut,),
        in_specs=[smem, smem, smem, take, take],
        out_specs=[give(s) for s in shapes] + [smem],
        out_shape=[jax.ShapeDtypeStruct(s, jnp.bfloat16) for s in shapes]
        + [jax.ShapeDtypeStruct((8,), jnp.int32)],
        scratch_shapes=[
            pltpu.SMEM((owner.shape[0],), jnp.int32),
            pltpu.SMEM((owner.shape[0],), jnp.int32),
            pltpu.SMEM((groups,), jnp.int32),
        ],
        compiler_params=pltpu.CompilerParams(vmem_limit_bytes=60 << 20),
        name="prepare",
    )(lengths, owner, table, one, two)


def dot_rows(x, y):
    return lax.dot_general(x, y, (((0,), (0,)), ((), ())), preferred_element_type=jnp.float32)


def symmetric_tiles(feat):
    return [((0, 0), (0, 1)), ((0, 2), (0, 3)), ((1, 2), (1, 3)), ((1, 1), (3, 3)), ((2, 2), (2, 3))]


def pack_symmetric(matrix):
    h = matrix.shape[0] // 4
    piece = lambda i, j: matrix[i * h : i * h + h, j * h : j * h + h]
    return [jnp.concatenate([piece(*p), piece(*q)], axis=1) for p, q in symmetric_tiles(4 * h)]


def pack_whole(matrix):
    h, half = matrix.shape[0] // 4, matrix.shape[1] // 2
    return [matrix[i * h : i * h + h, j * half : j * half + half] for i in range(4) for j in range(2)]


def stack_rows(refs, kind):
    return jnp.concatenate([ref[0, kind, 0] for ref in refs], axis=0)


def begin_kernel(column, meta, *refs):
    own, last, outs = refs[:4], refs[4:8], refs[8:]
    k = pl.program_id(0)

    @pl.when(k < KEEP)
    def _():
        for kind in range(2):
            f, l = stack_rows(own, kind), stack_rows(last, kind)
            outs[2 * kind][0] = dot_rows(f, f)
            outs[2 * kind + 1][0] = dot_rows(l, f)

    @pl.when(k >= KEEP)
    def _():
        for out in outs:
            out[...] = jnp.zeros_like(out)


def by_sender(shape, index_of):
    wide, _, _, rows, feat = shape

    def spec(back):
        def index(*args):
            kind, k = index_of(*args)
            return ((args[-2][0] + wide - back) % wide, kind, k, 0, 0)

        return index

    return [spec(back) for back in range(wide)]


def begin(column, meta, f_in, l_in):
    wide, kinds, _, rows, feat = f_in.shape
    low = lambda k, c, m: (0, jnp.minimum(k, KEEP - 1))
    both = (1, kinds, 1, rows, feat)
    received = lambda k, c, m: (0, 0, jnp.minimum(k, KEEP - 1), 0, 0)
    return pl.pallas_call(
        begin_kernel,
        grid_spec=pltpu.PrefetchScalarGridSpec(
            num_scalar_prefetch=2,
            grid=(2 * KEEP,),
            in_specs=[pl.BlockSpec(both, index) for index in by_sender(f_in.shape, low)]
            + [pl.BlockSpec(both, received)] * wide,
            out_specs=[pl.BlockSpec((1, feat, feat), lambda k, c, m: (k, 0, 0))] * 4,
        ),
        out_shape=[jax.ShapeDtypeStruct((2 * KEEP, feat, feat), jnp.float32)] * 4,
        compiler_params=pltpu.CompilerParams(vmem_limit_bytes=32 << 20),
        name="begin",
    )(column, meta, *[f_in] * wide, *l_in)


def finish_kernel(column, meta, *refs):
    first, last, sums, outs = (refs[n : n + 4] for n in range(0, 16, 4))
    ways, (packed, sem) = refs[16:18], refs[18:]
    kind, k = pl.program_id(0), pl.program_id(1)
    feat = last[0].shape[-1]
    spare = meta[0] != 0
    foreign = spare | ((meta[1] != 0) & (k == 1))
    f = jnp.concatenate([ref[0, 0, 0] for ref in first], axis=0)
    l = jnp.concatenate([ref[0, 0, 0] for ref in last], axis=0)
    both = dot_rows(jnp.concatenate([f, l], axis=1), f)

    def copies(way, which):
        return [
            pltpu.make_async_copy(
                packed.at[way, pl.ds(start, count)], ways[way].at[pl.ds(start, count)], sem.at[way, which, part]
            )
            for part, (start, count) in enumerate([(5 * which, 5), (10 + 8 * which, 8)])
        ]

    for which in range(2):

        @pl.when(kind == which)
        def _():
            factor = sums[2 * which][0] + both[:feat]
            between = sums[2 * which + 1][0] + both[feat:]
            outs[2 * which][0] = jnp.where(foreign, 0.0, factor)
            outs[2 * which + 1][0] = jnp.where(foreign, 0.0, between)
            for way, chosen in ((0, spare == (k == 0)), (1, k == 1)):

                @pl.when(foreign & chosen)
                def _():
                    for n, piece in enumerate(pack_symmetric(factor)):
                        packed[way, 5 * which + n] = piece.astype(jnp.bfloat16)
                    for n, piece in enumerate(pack_whole(between)):
                        packed[way, 10 + 8 * which + n] = piece.astype(jnp.bfloat16)
                    for copy in copies(way, which):
                        copy.start()

    @pl.when(foreign & (k == 1) & (kind == 1))
    def _():
        for way in range(2):
            for which in range(2):
                for copy in copies(way, which):
                    copy.wait()


def finish(column, meta, f_swap, l_in, sums):
    wide, _, _, rows, feat = f_swap.shape
    one = (1, 1, 1, rows, feat)
    here = lambda kind, k, c, m: (kind, k)
    own = [
        pl.BlockSpec((1, feat, feat), lambda kind, k, c, m: (jnp.where(kind == 0, k, KEEP - 1), 0, 0)),
        pl.BlockSpec((1, feat, feat), lambda kind, k, c, m: (jnp.where(kind == 1, k, 0), 0, 0)),
    ]
    blocks = [own[0], own[0], own[1], own[1]]
    way = jax.ShapeDtypeStruct((26, feat // 4, feat // 2), jnp.bfloat16)
    out = jax.ShapeDtypeStruct((2 * KEEP, feat, feat), jnp.float32)
    anywhere = pl.BlockSpec(memory_space=pl.ANY)
    return pl.pallas_call(
        finish_kernel,
        grid_spec=pltpu.PrefetchScalarGridSpec(
            num_scalar_prefetch=2,
            grid=(2, KEEP),
            in_specs=[pl.BlockSpec(one, index) for index in by_sender(f_swap.shape, here)]
            + [pl.BlockSpec(one, lambda kind, k, c, m: (0, kind, k, 0, 0))] * wide
            + blocks,
            out_specs=blocks + [anywhere] * 2,
            scratch_shapes=[
                pltpu.VMEM((2,) + way.shape, jnp.bfloat16),
                pltpu.SemaphoreType.DMA((2, 2, 2)),
            ],
        ),
        out_shape=[out] * 4 + [way] * 2,
        input_output_aliases={2 + 2 * wide + n: n for n in range(4)},
        compiler_params=pltpu.CompilerParams(vmem_limit_bytes=32 << 20),
        name="finish",
    )(column, meta, *[f_swap] * wide, *l_in, *sums)


def fill_kernel(meta, *refs):
    ways, outs, (half, wide, load_sem, store_sem) = refs[:2], refs[6:10], refs[10:]
    feat = wide.shape[-1]
    h = feat // 4
    slots = [meta[2], meta[3]]
    loads = [pltpu.make_async_copy(ways[w], half.at[w], load_sem.at[w]) for w in range(2)]

    def stores(w):
        return [
            pltpu.make_async_copy(wide.at[w, n], outs[n].at[slots[w]], store_sem.at[w, n]) for n in range(4)
        ]

    for w in range(2):

        @pl.when(slots[w] != 0)
        def _():
            loads[w].start()

    for w in range(2):

        @pl.when(slots[w] != 0)
        def _():
            loads[w].wait()
            started = stores(w)
            for kind in range(2):
                for n, pair in enumerate(symmetric_tiles(feat)):
                    for m, (i, j) in enumerate(pair):
                        piece = half[w, 5 * kind + n, :, m * h : m * h + h].astype(jnp.float32)
                        wide[w, 2 * kind, i * h : i * h + h, j * h : j * h + h] = piece
                        if i != j:
                            wide[w, 2 * kind, j * h : j * h + h, i * h : i * h + h] = piece.T
                started[2 * kind].start()
                for n in range(8):
                    i, j = n // 2, n % 2
                    piece = half[w, 10 + 8 * kind + n].astype(jnp.float32)
                    wide[w, 2 * kind + 1, i * h : i * h + h, 2 * j * h : 2 * j * h + 2 * h] = piece
                started[2 * kind + 1].start()

    for w in range(2):

        @pl.when(slots[w] != 0)
        def _():
            for store in stores(w):
                store.wait()


def fill(meta, way_a, way_b, outs):
    feat = outs[0].shape[-1]
    anywhere = pl.BlockSpec(memory_space=pl.ANY)
    return pl.pallas_call(
        fill_kernel,
        in_specs=[pl.BlockSpec(memory_space=pltpu.SMEM)] + [anywhere] * 6,
        out_specs=[anywhere] * 4,
        out_shape=[jax.ShapeDtypeStruct(o.shape, o.dtype) for o in outs],
        scratch_shapes=[
            pltpu.VMEM((2,) + way_a.shape, jnp.bfloat16),
            pltpu.VMEM((2, 4, feat, feat), jnp.float32),
            pltpu.SemaphoreType.DMA((2,)),
            pltpu.SemaphoreType.DMA((2, 4)),
        ],
        input_output_aliases={3 + n: n for n in range(4)},
        compiler_params=pltpu.CompilerParams(vmem_limit_bytes=60 << 20),
        name="fill_slots",
    )(meta, way_a, way_b, *outs)


def hand_over(route, groups, way_a, way_b):
    sections = lax.axis_size("section")

    def along(number, *values):
        sent = []
        for value, step in zip(values, patterns(number)):
            pairs = [(s * groups + i, s * groups + j) for s in range(sections) for i, j in step.items()]
            sent.append(lax.ppermute(value, AXES, pairs))
        return tuple(sent)

    return lax.switch(route, [functools.partial(along, n) for n in range(groups + 1)], way_a, way_b)


def on_device(first_acts, first_grads, last_acts, last_grads, doc_lengths, block_owner):
    groups = lax.axis_size("dp")
    sections = lax.axis_size("section")
    table = jnp.asarray(plan_table(groups))
    column = (lax.axis_index("dp") // 2).astype(jnp.int32).reshape(1)
    f_own, f_other, meta = prepare(doc_lengths, block_owner, table, first_acts[0], first_grads[0], groups, False)
    meta, last_acts, last_grads = lax.optimization_barrier((meta, last_acts, last_grads))
    l_own, l_other, _ = prepare(doc_lengths, block_owner, table, last_acts[0], last_grads[0], groups, True)

    straight = [(s * groups + d, (s + 1) * groups + d) for s in range(sections - 1) for d in range(groups)]
    across = [(i, j ^ 1) for i, j in straight]
    swap = [(i, i ^ 1) for i in range(sections * groups)]
    rows_of = [[d for d in range(groups) if d % 2 == y] for y in range(2)]

    def exchange(x):
        return lax.all_to_all(x, "dp", split_axis=0, concat_axis=0, tiled=True, axis_index_groups=rows_of)

    def spread(x):
        turns = [[(i, i // groups * groups + (i + 2 * n) % groups) for i in range(sections * groups)] for n in range(4)]
        return [x] + [lax.ppermute(x[n : n + 1], AXES, turns[n]) for n in range(1, 4)]

    l_own = lax.ppermute(l_own, AXES, straight)
    l_other = lax.ppermute(l_other, AXES, across)
    f_other = exchange(f_other)
    f_other, f_own = lax.optimization_barrier((f_other, f_own))
    f_swap = lax.ppermute(f_other, AXES, swap)
    f_own = exchange(f_own)
    l_own = spread(l_own)
    l_other = spread(l_other)
    sums = begin(column, meta, f_own, l_own)
    af, ac, gf, gc, *ways = finish(column, meta, f_swap, l_other, sums)
    got = hand_over(meta[4], groups, *ways)
    af, ac, gf, gc = fill(meta, *got, (af, ac, gf, gc))
    return af[None, None], gf[None, None], ac[None, None], gc[None, None]


def solution(mesh):
    placed = (
        P("section", "dp", None),
        P("section", "dp", None),
        P("section", "dp", None),
        P("section", "dp", None),
        P("dp", None),
        P(),
    )
    return jax.shard_map(
        on_device,
        mesh=mesh,
        in_specs=placed,
        out_specs=(P("section", "dp", None, None, None),) * 4,
        check_vma=False,
    )
```

```python
import functools

import jax
import jax.numpy as jnp
import numpy as np
from jax import lax
from jax.experimental import pallas as pl
from jax.experimental.pallas import tpu as pltpu
from jax.sharding import PartitionSpec as P

KEEP = 2
AXES = ("section", "dp")


def at(x, y):
    return (x % 4) * 2 + y


def patterns(route):
    if route == 0:
        return [{at(x, y): at(x + step, y) for x in range(4) for y in range(2)} for step in (1, -1)]
    xf, yf = (route - 1) // 2, (route - 1) % 2
    near = 1 - yf
    plus = {at(x, near): at(x + 1, near) for x in range(4)}
    plus[at(xf, near)] = at(xf, yf)
    minus = {at(x, near): at(x - 1, near) for x in range(4)}
    minus[at(xf + 1, near)] = at(xf + 1, yf)
    minus[at(xf + 1, yf)] = at(xf, yf)
    return [plus, minus]


def chains(spare, full):
    ways = []
    for step in patterns(0 if spare % 2 == full % 2 else 1 + full):
        between = [step[spare]]
        while between[-1] != full:
            between.append(step[between[-1]])
        ways.append(between[:-1])
    return ways


def plan_table(groups):
    table = np.zeros((groups * groups, 16), np.int32)
    for spare, full in [(s, f) for s in range(1, groups - 1) for f in range(groups) if f != s]:
        row = table[spare * groups + full]
        row[:groups] = np.arange(groups) * KEEP + 1
        for way, between in enumerate(chains(spare, full)):
            slot = spare * KEEP + way
            for g in between:
                row[g] = slot
                slot = g * KEEP + 1
                row[groups + 2 + way] |= 1 << g
            row[groups + way] = slot
        row[groups + 4] = 0 if spare % 2 == full % 2 else 1 + full
    return table.reshape(-1)


def prepare_kernel(groups, relative, lengths, owner, table, one, two, *refs):
    outs, (meta, order, slots, counts) = refs[:-4], refs[-4:]
    blocks = owner.shape[0]
    step = pl.program_id(0)
    me = lax.axis_index("dp")

    @pl.when(step == 0)
    def _():
        for g in range(groups):
            counts[g] = 0
        for b in range(blocks):
            o = owner[b]
            slots[b] = counts[o]
            counts[o] = counts[o] + 1
        spare, full = jnp.int32(0), jnp.int32(0)
        for g in range(groups):
            spare = jnp.where(counts[g] == 0, g, spare)
            full = jnp.where(counts[g] > KEEP, g, full)
        row = (spare * groups + full) * 16
        for b in range(blocks):
            o, k = owner[b], slots[b]
            at = jnp.where(k <= 1, o, groups + jnp.minimum(k, 3) - 2)
            place = jnp.where(k == 0, o * KEEP, table[row + at])
            order[place] = b
        on_a = (table[row + groups + 2] >> me) & 1
        on_b = (table[row + groups + 3] >> me) & 1
        last = (me == full).astype(jnp.int32)
        meta[0] = (me == spare).astype(jnp.int32)
        meta[1] = on_a | on_b
        meta[2] = on_a + 2 * last
        meta[3] = on_b + 3 * last
        meta[4] = table[row + groups + 4]

    rows, width = one.shape
    feat = width // blocks
    lanes = 128
    row_at = lax.broadcasted_iota(jnp.int32, (rows, lanes), 0) + step * rows
    length = jnp.ones((rows, lanes), jnp.float32)
    start = jnp.int32(0)
    for d in range(lengths.shape[1]):
        size = lengths[0, d]
        inside = (row_at >= start) & (row_at < start + size)
        length = jnp.where(inside, size.astype(jnp.float32), length)
        start = start + size
    weight = jnp.sqrt((1.0 / length) / (lengths.shape[1] * groups))
    weight = jnp.concatenate([weight] * (feat // lanes), axis=1)
    half = me % 2
    for x in range(groups // 2):
        for t in range(2):
            for k in range(KEEP):
                column = (me // 2 + x) % 4 if relative else x
                source = order[column * 4 + (half ^ t) * KEEP + k]
                columns = pl.ds(pl.multiple_of(source * feat, feat), feat)
                for a, ref in ((0, one), (1, two)):
                    value = (ref[:, columns].astype(jnp.float32) * weight).astype(jnp.bfloat16)
                    outs[t][x, a, k] = value


def prepare(lengths, owner, table, one, two, groups, relative):
    rows, width = one.shape
    feat = width // owner.shape[0]
    cut = rows // 2
    wide = groups // 2
    shapes = [(wide, 2, KEEP, rows, feat)] * 2
    smem = pl.BlockSpec(memory_space=pltpu.SMEM)
    take = pl.BlockSpec((cut, width), lambda i: (i, 0))

    def give(shape):
        lead = len(shape) - 2
        return pl.BlockSpec(shape[:lead] + (cut, feat), lambda i: (0,) * lead + (i, 0))

    return pl.pallas_call(
        functools.partial(prepare_kernel, groups, relative),
        grid=(rows // cut,),
        in_specs=[smem, smem, smem, take, take],
        out_specs=[give(s) for s in shapes] + [smem],
        out_shape=[jax.ShapeDtypeStruct(s, jnp.bfloat16) for s in shapes]
        + [jax.ShapeDtypeStruct((8,), jnp.int32)],
        scratch_shapes=[
            pltpu.SMEM((owner.shape[0],), jnp.int32),
            pltpu.SMEM((owner.shape[0],), jnp.int32),
            pltpu.SMEM((groups,), jnp.int32),
        ],
        compiler_params=pltpu.CompilerParams(vmem_limit_bytes=60 << 20),
        name="prepare",
    )(lengths, owner, table, one, two)


def dot_rows(x, y):
    return lax.dot_general(x, y, (((0,), (0,)), ((), ())), preferred_element_type=jnp.float32)


def symmetric_tiles(feat):
    return [((0, 0), (0, 1)), ((0, 2), (0, 3)), ((1, 2), (1, 3)), ((1, 1), (3, 3)), ((2, 2), (2, 3))]


def pack_symmetric(matrix):
    h = matrix.shape[0] // 4
    piece = lambda i, j: matrix[i * h : i * h + h, j * h : j * h + h]
    return [jnp.concatenate([piece(*p), piece(*q)], axis=1) for p, q in symmetric_tiles(4 * h)]


def pack_whole(matrix):
    h, half = matrix.shape[0] // 4, matrix.shape[1] // 2
    return [matrix[i * h : i * h + h, j * half : j * half + half] for i in range(4) for j in range(2)]


def stack_rows(refs, kind):
    return jnp.concatenate([ref[0, kind, 0] for ref in refs], axis=0)


def begin_kernel(column, meta, *refs):
    own, last, outs = refs[:4], refs[4:8], refs[8:]
    k = pl.program_id(0)

    @pl.when(k < KEEP)
    def _():
        for kind in range(2):
            f, l = stack_rows(own, kind), stack_rows(last, kind)
            outs[2 * kind][0] = dot_rows(f, f)
            outs[2 * kind + 1][0] = dot_rows(l, f)

    @pl.when(k >= KEEP)
    def _():
        for out in outs:
            out[...] = jnp.zeros_like(out)


def by_sender(shape, index_of):
    wide, _, _, rows, feat = shape

    def spec(back):
        def index(*args):
            kind, k = index_of(*args)
            return ((args[-2][0] + wide - back) % wide, kind, k, 0, 0)

        return index

    return [spec(back) for back in range(wide)]


def begin(column, meta, f_in, l_in):
    wide, kinds, _, rows, feat = f_in.shape
    low = lambda k, c, m: (0, jnp.minimum(k, KEEP - 1))
    both = (1, kinds, 1, rows, feat)
    received = lambda k, c, m: (0, 0, jnp.minimum(k, KEEP - 1), 0, 0)
    return pl.pallas_call(
        begin_kernel,
        grid_spec=pltpu.PrefetchScalarGridSpec(
            num_scalar_prefetch=2,
            grid=(2 * KEEP,),
            in_specs=[pl.BlockSpec(both, index) for index in by_sender(f_in.shape, low)]
            + [pl.BlockSpec(both, received)] * wide,
            out_specs=[pl.BlockSpec((1, feat, feat), lambda k, c, m: (k, 0, 0))] * 4,
        ),
        out_shape=[jax.ShapeDtypeStruct((2 * KEEP, feat, feat), jnp.float32)] * 4,
        compiler_params=pltpu.CompilerParams(vmem_limit_bytes=32 << 20),
        name="begin",
    )(column, meta, *[f_in] * wide, *l_in)


def finish_kernel(column, meta, *refs):
    first, last, sums, outs = (refs[n : n + 4] for n in range(0, 16, 4))
    ways, (packed, sem) = refs[16:18], refs[18:]
    kind, k = pl.program_id(0), pl.program_id(1)
    feat = last[0].shape[-1]
    spare = meta[0] != 0
    foreign = spare | ((meta[1] != 0) & (k == 1))
    f = jnp.concatenate([ref[0, 0, 0] for ref in first], axis=0)
    l = jnp.concatenate([ref[0, 0, 0] for ref in last], axis=0)
    both = dot_rows(jnp.concatenate([f, l], axis=1), f)

    def copies(way, which):
        return [
            pltpu.make_async_copy(
                packed.at[way, pl.ds(start, count)], ways[way].at[pl.ds(start, count)], sem.at[way, which, part]
            )
            for part, (start, count) in enumerate([(5 * which, 5), (10 + 8 * which, 8)])
        ]

    for which in range(2):

        @pl.when(kind == which)
        def _():
            factor = sums[2 * which][0] + both[:feat]
            between = sums[2 * which + 1][0] + both[feat:]
            outs[2 * which][0] = jnp.where(foreign, 0.0, factor)
            outs[2 * which + 1][0] = jnp.where(foreign, 0.0, between)
            for way, chosen in ((0, spare == (k == 0)), (1, k == 1)):

                @pl.when(foreign & chosen)
                def _():
                    for n, piece in enumerate(pack_symmetric(factor)):
                        packed[way, 5 * which + n] = piece.astype(jnp.bfloat16)
                    for n, piece in enumerate(pack_whole(between)):
                        packed[way, 10 + 8 * which + n] = piece.astype(jnp.bfloat16)
                    for copy in copies(way, which):
                        copy.start()

    @pl.when(foreign & (k == 1) & (kind == 1))
    def _():
        for way in range(2):
            for which in range(2):
                for copy in copies(way, which):
                    copy.wait()


def finish(column, meta, f_swap, l_in, sums):
    wide, _, _, rows, feat = f_swap.shape
    one = (1, 1, 1, rows, feat)
    here = lambda kind, k, c, m: (kind, k)
    own = [
        pl.BlockSpec((1, feat, feat), lambda kind, k, c, m: (jnp.where(kind == 0, k, KEEP - 1), 0, 0)),
        pl.BlockSpec((1, feat, feat), lambda kind, k, c, m: (jnp.where(kind == 1, k, 0), 0, 0)),
    ]
    blocks = [own[0], own[0], own[1], own[1]]
    way = jax.ShapeDtypeStruct((26, feat // 4, feat // 2), jnp.bfloat16)
    out = jax.ShapeDtypeStruct((2 * KEEP, feat, feat), jnp.float32)
    anywhere = pl.BlockSpec(memory_space=pl.ANY)
    return pl.pallas_call(
        finish_kernel,
        grid_spec=pltpu.PrefetchScalarGridSpec(
            num_scalar_prefetch=2,
            grid=(2, KEEP),
            in_specs=[pl.BlockSpec(one, index) for index in by_sender(f_swap.shape, here)]
            + [pl.BlockSpec(one, lambda kind, k, c, m: (0, kind, k, 0, 0))] * wide
            + blocks,
            out_specs=blocks + [anywhere] * 2,
            scratch_shapes=[
                pltpu.VMEM((2,) + way.shape, jnp.bfloat16),
                pltpu.SemaphoreType.DMA((2, 2, 2)),
            ],
        ),
        out_shape=[out] * 4 + [way] * 2,
        input_output_aliases={2 + 2 * wide + n: n for n in range(4)},
        compiler_params=pltpu.CompilerParams(vmem_limit_bytes=32 << 20),
        name="finish",
    )(column, meta, *[f_swap] * wide, *l_in, *sums)


def fill_kernel(meta, *refs):
    ways, outs, (half, wide, load_sem, store_sem) = refs[:2], refs[6:10], refs[10:]
    feat = wide.shape[-1]
    h = feat // 4
    slots = [meta[2], meta[3]]
    loads = [pltpu.make_async_copy(ways[w], half.at[w], load_sem.at[w]) for w in range(2)]

    def stores(w):
        return [
            pltpu.make_async_copy(wide.at[w, n], outs[n].at[slots[w]], store_sem.at[w, n]) for n in range(4)
        ]

    for w in range(2):

        @pl.when(slots[w] != 0)
        def _():
            loads[w].start()

    for w in range(2):

        @pl.when(slots[w] != 0)
        def _():
            loads[w].wait()
            started = stores(w)
            for kind in range(2):
                for n, pair in enumerate(symmetric_tiles(feat)):
                    for m, (i, j) in enumerate(pair):
                        piece = half[w, 5 * kind + n, :, m * h : m * h + h].astype(jnp.float32)
                        wide[w, 2 * kind, i * h : i * h + h, j * h : j * h + h] = piece
                        if i != j:
                            wide[w, 2 * kind, j * h : j * h + h, i * h : i * h + h] = piece.T
                started[2 * kind].start()
                for n in range(8):
                    i, j = n // 2, n % 2
                    piece = half[w, 10 + 8 * kind + n].astype(jnp.float32)
                    wide[w, 2 * kind + 1, i * h : i * h + h, 2 * j * h : 2 * j * h + 2 * h] = piece
                started[2 * kind + 1].start()

    for w in range(2):

        @pl.when(slots[w] != 0)
        def _():
            for store in stores(w):
                store.wait()


def fill(meta, way_a, way_b, outs):
    feat = outs[0].shape[-1]
    anywhere = pl.BlockSpec(memory_space=pl.ANY)
    return pl.pallas_call(
        fill_kernel,
        in_specs=[pl.BlockSpec(memory_space=pltpu.SMEM)] + [anywhere] * 6,
        out_specs=[anywhere] * 4,
        out_shape=[jax.ShapeDtypeStruct(o.shape, o.dtype) for o in outs],
        scratch_shapes=[
            pltpu.VMEM((2,) + way_a.shape, jnp.bfloat16),
            pltpu.VMEM((2, 4, feat, feat), jnp.float32),
            pltpu.SemaphoreType.DMA((2,)),
            pltpu.SemaphoreType.DMA((2, 4)),
        ],
        input_output_aliases={3 + n: n for n in range(4)},
        compiler_params=pltpu.CompilerParams(vmem_limit_bytes=60 << 20),
        name="fill_slots",
    )(meta, way_a, way_b, *outs)


def hand_over(route, groups, way_a, way_b):
    sections = lax.axis_size("section")

    def along(number, *values):
        sent = []
        for value, step in zip(values, patterns(number)):
            pairs = [(s * groups + i, s * groups + j) for s in range(sections) for i, j in step.items()]
            sent.append(lax.ppermute(value, AXES, pairs))
        return tuple(sent)

    return lax.switch(route, [functools.partial(along, n) for n in range(groups + 1)], way_a, way_b)


def on_device(first_acts, first_grads, last_acts, last_grads, doc_lengths, block_owner):
    groups = lax.axis_size("dp")
    sections = lax.axis_size("section")
    table = jnp.asarray(plan_table(groups))
    column = (lax.axis_index("dp") // 2).astype(jnp.int32).reshape(1)
    f_own, f_other, meta = prepare(doc_lengths, block_owner, table, first_acts[0], first_grads[0], groups, False)
    meta, last_acts, last_grads = lax.optimization_barrier((meta, last_acts, last_grads))
    l_own, l_other, _ = prepare(doc_lengths, block_owner, table, last_acts[0], last_grads[0], groups, True)

    straight = [(s * groups + d, (s + 1) * groups + d) for s in range(sections - 1) for d in range(groups)]
    across = [(i, j ^ 1) for i, j in straight]
    swap = [(i, i ^ 1) for i in range(sections * groups)]
    rows_of = [[d for d in range(groups) if d % 2 == y] for y in range(2)]

    def exchange(x):
        return lax.all_to_all(x, "dp", split_axis=0, concat_axis=0, tiled=True, axis_index_groups=rows_of)

    def spread(x):
        turns = [[(i, i // groups * groups + (i + 2 * n) % groups) for i in range(sections * groups)] for n in range(4)]
        return [x] + [lax.ppermute(x[n : n + 1], AXES, turns[n]) for n in range(1, 4)]

    l_own = lax.ppermute(l_own, AXES, straight)
    l_other = lax.ppermute(l_other, AXES, across)
    f_other = exchange(f_other)
    f_other, f_own = lax.optimization_barrier((f_other, f_own))
    f_swap = lax.ppermute(f_other, AXES, swap)
    f_own = exchange(f_own)
    l_own = spread(l_own)
    l_other = spread(l_other)
    sums = begin(column, meta, f_own, l_own)
    af, ac, gf, gc, *ways = finish(column, meta, f_swap, l_other, sums)
    got = hand_over(meta[4], groups, *ways)
    af, ac, gf, gc = fill(meta, *got, (af, ac, gf, gc))
    return af[None, None], gf[None, None], ac[None, None], gc[None, None]


def solution(mesh):
    placed = (
        P("section", "dp", None),
        P("section", "dp", None),
        P("section", "dp", None),
        P("section", "dp", None),
        P("dp", None),
        P(),
    )
    return jax.shard_map(
        on_device,
        mesh=mesh,
        in_specs=placed,
        out_specs=(P("section", "dp", None, None, None),) * 4,
        check_vma=False,
    )
```

```python
import functools

import jax
import jax.numpy as jnp
import numpy as np
from jax import lax
from jax.experimental import pallas as pl
from jax.experimental.pallas import tpu as pltpu
from jax.sharding import PartitionSpec as P

KEEP = 2
AXES = ("section", "dp")


def at(x, y):
    return (x % 4) * 2 + y


def patterns(route):
    if route == 0:
        return [{at(x, y): at(x + step, y) for x in range(4) for y in range(2)} for step in (1, -1)]
    xf, yf = (route - 1) // 2, (route - 1) % 2
    near = 1 - yf
    plus = {at(x, near): at(x + 1, near) for x in range(4)}
    plus[at(xf, near)] = at(xf, yf)
    minus = {at(x, near): at(x - 1, near) for x in range(4)}
    minus[at(xf + 1, near)] = at(xf + 1, yf)
    minus[at(xf + 1, yf)] = at(xf, yf)
    return [plus, minus]


def chains(spare, full):
    ways = []
    for step in patterns(0 if spare % 2 == full % 2 else 1 + full):
        between = [step[spare]]
        while between[-1] != full:
            between.append(step[between[-1]])
        ways.append(between[:-1])
    return ways


def plan_table(groups):
    table = np.zeros((groups * groups, 16), np.int32)
    for spare, full in [(s, f) for s in range(1, groups - 1) for f in range(groups) if f != s]:
        row = table[spare * groups + full]
        row[:groups] = np.arange(groups) * KEEP + 1
        for way, between in enumerate(chains(spare, full)):
            slot = spare * KEEP + way
            for g in between:
                row[g] = slot
                slot = g * KEEP + 1
                row[groups + 2 + way] |= 1 << g
            row[groups + way] = slot
        row[groups + 4] = 0 if spare % 2 == full % 2 else 1 + full
    return table.reshape(-1)


def prepare_kernel(groups, apart, lengths, owner, table, one, two, *refs):
    outs, (meta, order, slots, counts) = refs[:-4], refs[-4:]
    blocks = owner.shape[0]
    step = pl.program_id(0)
    me = lax.axis_index("dp")

    @pl.when(step == 0)
    def _():
        for g in range(groups):
            counts[g] = 0
        for b in range(blocks):
            o = owner[b]
            slots[b] = counts[o]
            counts[o] = counts[o] + 1
        spare, full = jnp.int32(0), jnp.int32(0)
        for g in range(groups):
            spare = jnp.where(counts[g] == 0, g, spare)
            full = jnp.where(counts[g] > KEEP, g, full)
        row = (spare * groups + full) * 16
        for b in range(blocks):
            o, k = owner[b], slots[b]
            at = jnp.where(k <= 1, o, groups + jnp.minimum(k, 3) - 2)
            place = jnp.where(k == 0, o * KEEP, table[row + at])
            order[place] = b
        on_a = (table[row + groups + 2] >> me) & 1
        on_b = (table[row + groups + 3] >> me) & 1
        last = (me == full).astype(jnp.int32)
        meta[0] = (me == spare).astype(jnp.int32)
        meta[1] = on_a | on_b
        meta[2] = on_a + 2 * last
        meta[3] = on_b + 3 * last
        meta[4] = table[row + groups + 4]

    rows, width = one.shape
    feat = width // blocks
    lanes = 128
    row_at = lax.broadcasted_iota(jnp.int32, (rows, lanes), 0) + step * rows
    length = jnp.ones((rows, lanes), jnp.float32)
    start = jnp.int32(0)
    for d in range(lengths.shape[1]):
        size = lengths[0, d]
        inside = (row_at >= start) & (row_at < start + size)
        length = jnp.where(inside, size.astype(jnp.float32), length)
        start = start + size
    weight = jnp.sqrt((1.0 / length) / (lengths.shape[1] * groups))
    weight = jnp.concatenate([weight] * (feat // lanes), axis=1)
    half = me % 2
    for x in range(groups // 2):
        for t in range(2):
            for k in range(KEEP):
                column = (me // 2 + x) % 4
                source = order[column * 4 + (half ^ t) * KEEP + k]
                columns = pl.ds(pl.multiple_of(source * feat, feat), feat)
                for a, ref in ((0, one), (1, two)):
                    value = (ref[:, columns].astype(jnp.float32) * weight).astype(jnp.bfloat16)
                    if apart:
                        outs[4 * t + x][0, a, k] = value
                    else:
                        outs[t][x, a, k] = value


def prepare(lengths, owner, table, one, two, groups, apart):
    rows, width = one.shape
    feat = width // owner.shape[0]
    cut = rows // 2
    wide = groups // 2
    shapes = [(1, 2, KEEP, rows, feat)] * 2 * wide if apart else [(wide, 2, KEEP, rows, feat)] * 2
    smem = pl.BlockSpec(memory_space=pltpu.SMEM)
    take = pl.BlockSpec((cut, width), lambda i: (i, 0))

    def give(shape):
        lead = len(shape) - 2
        return pl.BlockSpec(shape[:lead] + (cut, feat), lambda i: (0,) * lead + (i, 0))

    return pl.pallas_call(
        functools.partial(prepare_kernel, groups, apart),
        grid=(rows // cut,),
        in_specs=[smem, smem, smem, take, take],
        out_specs=[give(s) for s in shapes] + [smem],
        out_shape=[jax.ShapeDtypeStruct(s, jnp.bfloat16) for s in shapes]
        + [jax.ShapeDtypeStruct((8,), jnp.int32)],
        scratch_shapes=[
            pltpu.SMEM((owner.shape[0],), jnp.int32),
            pltpu.SMEM((owner.shape[0],), jnp.int32),
            pltpu.SMEM((groups,), jnp.int32),
        ],
        compiler_params=pltpu.CompilerParams(vmem_limit_bytes=60 << 20),
        name="prepare",
    )(lengths, owner, table, one, two)


def dot_rows(x, y):
    return lax.dot_general(x, y, (((0,), (0,)), ((), ())), preferred_element_type=jnp.float32)


def symmetric_tiles(feat):
    return [((0, 0), (0, 1)), ((0, 2), (0, 3)), ((1, 2), (1, 3)), ((1, 1), (3, 3)), ((2, 2), (2, 3))]


def pack_symmetric(matrix):
    h = matrix.shape[0] // 4
    piece = lambda i, j: matrix[i * h : i * h + h, j * h : j * h + h]
    return [jnp.concatenate([piece(*p), piece(*q)], axis=1) for p, q in symmetric_tiles(4 * h)]


def pack_whole(matrix):
    h, half = matrix.shape[0] // 4, matrix.shape[1] // 2
    return [matrix[i * h : i * h + h, j * half : j * half + half] for i in range(4) for j in range(2)]


def stack_rows(refs, kind):
    return jnp.concatenate([ref[0, kind, 0] for ref in refs], axis=0)


def begin_kernel(*refs):
    own, last, outs = refs[:4], refs[4:8], refs[8:]
    k = pl.program_id(0)

    @pl.when(k < KEEP)
    def _():
        for kind in range(2):
            f, l = stack_rows(own, kind), stack_rows(last, kind)
            outs[2 * kind][0] = dot_rows(f, f)
            outs[2 * kind + 1][0] = dot_rows(l, f)

    @pl.when(k >= KEEP)
    def _():
        for out in outs:
            out[...] = jnp.zeros_like(out)


def begin(f_in, l_in):
    _, kinds, _, rows, feat = f_in[0].shape
    received = pl.BlockSpec((1, kinds, 1, rows, feat), lambda k: (0, 0, jnp.minimum(k, KEEP - 1), 0, 0))
    return pl.pallas_call(
        begin_kernel,
        grid=(2 * KEEP,),
        in_specs=[received] * 8,
        out_specs=[pl.BlockSpec((1, feat, feat), lambda k: (k, 0, 0))] * 4,
        out_shape=[jax.ShapeDtypeStruct((2 * KEEP, feat, feat), jnp.float32)] * 4,
        compiler_params=pltpu.CompilerParams(vmem_limit_bytes=32 << 20),
        name="begin",
    )(*f_in, *l_in)


def finish_kernel(meta, *refs):
    first, last, sums, outs = (refs[n : n + 4] for n in range(0, 16, 4))
    ways, (packed, sem) = refs[16:18], refs[18:]
    kind, k = pl.program_id(0), pl.program_id(1)
    feat = last[0].shape[-1]
    spare = meta[0] != 0
    foreign = spare | ((meta[1] != 0) & (k == 1))
    f = jnp.concatenate([ref[0, 0, 0] for ref in first], axis=0)
    l = jnp.concatenate([ref[0, 0, 0] for ref in last], axis=0)
    both = dot_rows(jnp.concatenate([f, l], axis=1), f)

    def copies(way, which):
        return [
            pltpu.make_async_copy(
                packed.at[way, pl.ds(start, count)], ways[way].at[pl.ds(start, count)], sem.at[way, which, part]
            )
            for part, (start, count) in enumerate([(5 * which, 5), (10 + 8 * which, 8)])
        ]

    for which in range(2):

        @pl.when(kind == which)
        def _():
            factor = sums[2 * which][0] + both[:feat]
            between = sums[2 * which + 1][0] + both[feat:]
            outs[2 * which][0] = jnp.where(foreign, 0.0, factor)
            outs[2 * which + 1][0] = jnp.where(foreign, 0.0, between)
            for way, chosen in ((0, spare == (k == 0)), (1, k == 1)):

                @pl.when(foreign & chosen)
                def _():
                    for n, piece in enumerate(pack_symmetric(factor)):
                        packed[way, 5 * which + n] = piece.astype(jnp.bfloat16)
                    for n, piece in enumerate(pack_whole(between)):
                        packed[way, 10 + 8 * which + n] = piece.astype(jnp.bfloat16)
                    for copy in copies(way, which):
                        copy.start()

    @pl.when(foreign & (k == 1) & (kind == 1))
    def _():
        for way in range(2):
            for which in range(2):
                for copy in copies(way, which):
                    copy.wait()


def finish(meta, f_swap, l_in, sums):
    _, _, _, rows, feat = f_swap[0].shape
    one = (1, 1, 1, rows, feat)
    received = pl.BlockSpec(one, lambda kind, k, m: (0, kind, k, 0, 0))
    own = [
        pl.BlockSpec((1, feat, feat), lambda kind, k, m: (jnp.where(kind == 0, k, KEEP - 1), 0, 0)),
        pl.BlockSpec((1, feat, feat), lambda kind, k, m: (jnp.where(kind == 1, k, 0), 0, 0)),
    ]
    blocks = [own[0], own[0], own[1], own[1]]
    way = jax.ShapeDtypeStruct((26, feat // 4, feat // 2), jnp.bfloat16)
    out = jax.ShapeDtypeStruct((2 * KEEP, feat, feat), jnp.float32)
    anywhere = pl.BlockSpec(memory_space=pl.ANY)
    return pl.pallas_call(
        finish_kernel,
        grid_spec=pltpu.PrefetchScalarGridSpec(
            num_scalar_prefetch=1,
            grid=(2, KEEP),
            in_specs=[received] * 8 + blocks,
            out_specs=blocks + [anywhere] * 2,
            scratch_shapes=[
                pltpu.VMEM((2,) + way.shape, jnp.bfloat16),
                pltpu.SemaphoreType.DMA((2, 2, 2)),
            ],
        ),
        out_shape=[out] * 4 + [way] * 2,
        input_output_aliases={9 + n: n for n in range(4)},
        compiler_params=pltpu.CompilerParams(vmem_limit_bytes=32 << 20),
        name="finish",
    )(meta, *f_swap, *l_in, *sums)


def fill_kernel(meta, *refs):
    ways, outs, (half, wide, load_sem, store_sem) = refs[:2], refs[6:10], refs[10:]
    feat = wide.shape[-1]
    h = feat // 4
    slots = [meta[2], meta[3]]
    loads = [pltpu.make_async_copy(ways[w], half.at[w], load_sem.at[w]) for w in range(2)]

    def stores(w):
        return [
            pltpu.make_async_copy(wide.at[w, n], outs[n].at[slots[w]], store_sem.at[w, n]) for n in range(4)
        ]

    for w in range(2):

        @pl.when(slots[w] != 0)
        def _():
            loads[w].start()

    for w in range(2):

        @pl.when(slots[w] != 0)
        def _():
            loads[w].wait()
            started = stores(w)
            for kind in range(2):
                for n, pair in enumerate(symmetric_tiles(feat)):
                    for m, (i, j) in enumerate(pair):
                        piece = half[w, 5 * kind + n, :, m * h : m * h + h].astype(jnp.float32)
                        wide[w, 2 * kind, i * h : i * h + h, j * h : j * h + h] = piece
                        if i != j:
                            wide[w, 2 * kind, j * h : j * h + h, i * h : i * h + h] = piece.T
                started[2 * kind].start()
                for n in range(8):
                    i, j = n // 2, n % 2
                    piece = half[w, 10 + 8 * kind + n].astype(jnp.float32)
                    wide[w, 2 * kind + 1, i * h : i * h + h, 2 * j * h : 2 * j * h + 2 * h] = piece
                started[2 * kind + 1].start()

    for w in range(2):

        @pl.when(slots[w] != 0)
        def _():
            for store in stores(w):
                store.wait()


def fill(meta, way_a, way_b, outs):
    feat = outs[0].shape[-1]
    anywhere = pl.BlockSpec(memory_space=pl.ANY)
    return pl.pallas_call(
        fill_kernel,
        in_specs=[pl.BlockSpec(memory_space=pltpu.SMEM)] + [anywhere] * 6,
        out_specs=[anywhere] * 4,
        out_shape=[jax.ShapeDtypeStruct(o.shape, o.dtype) for o in outs],
        scratch_shapes=[
            pltpu.VMEM((2,) + way_a.shape, jnp.bfloat16),
            pltpu.VMEM((2, 4, feat, feat), jnp.float32),
            pltpu.SemaphoreType.DMA((2,)),
            pltpu.SemaphoreType.DMA((2, 4)),
        ],
        input_output_aliases={3 + n: n for n in range(4)},
        compiler_params=pltpu.CompilerParams(vmem_limit_bytes=60 << 20),
        name="fill_slots",
    )(meta, way_a, way_b, *outs)


def hand_over(route, groups, way_a, way_b):
    sections = lax.axis_size("section")

    def along(number, *values):
        sent = []
        for value, step in zip(values, patterns(number)):
            pairs = [(s * groups + i, s * groups + j) for s in range(sections) for i, j in step.items()]
            sent.append(lax.ppermute(value, AXES, pairs))
        return tuple(sent)

    return lax.switch(route, [functools.partial(along, n) for n in range(groups + 1)], way_a, way_b)


def on_device(first_acts, first_grads, last_acts, last_grads, doc_lengths, block_owner):
    groups = lax.axis_size("dp")
    sections = lax.axis_size("section")
    table = jnp.asarray(plan_table(groups))
    l_own, l_other, meta = prepare(doc_lengths, block_owner, table, last_acts[0], last_grads[0], groups, False)
    meta, first_acts, first_grads = lax.optimization_barrier((meta, first_acts, first_grads))
    *f, _ = prepare(doc_lengths, block_owner, table, first_acts[0], first_grads[0], groups, True)

    straight = [(s * groups + d, (s + 1) * groups + d) for s in range(sections - 1) for d in range(groups)]
    across = [(i, j ^ 1) for i, j in straight]
    swap = [(i, i ^ 1) for i in range(sections * groups)]
    turns = [[(i, i // groups * groups + (i + 2 * n) % groups) for i in range(sections * groups)] for n in range(4)]

    def spread(parts):
        return [parts[0]] + [lax.ppermute(parts[n], AXES, turns[n]) for n in range(1, 4)]

    def cut(x):
        return [x] + [x[n : n + 1] for n in range(1, 4)]

    f_other = spread(f[4:])
    f_own, f_other = lax.optimization_barrier((f[:4], f_other))
    f_own = spread(f_own)
    l_own = spread(cut(lax.ppermute(l_own, AXES, straight)))
    l_other = spread(cut(lax.ppermute(l_other, AXES, across)))
    f_swap = [lax.ppermute(part, AXES, swap) for part in f[4:5] + f_other[1:]]
    sums = begin(f_own, l_own)
    af, ac, gf, gc, *ways = finish(meta, f_swap, l_other, sums)
    got = hand_over(meta[4], groups, *ways)
    af, ac, gf, gc = fill(meta, *got, (af, ac, gf, gc))
    return af[None, None], gf[None, None], ac[None, None], gc[None, None]


def solution(mesh):
    placed = (
        P("section", "dp", None),
        P("section", "dp", None),
        P("section", "dp", None),
        P("section", "dp", None),
        P("dp", None),
        P(),
    )
    return jax.shard_map(
        on_device,
        mesh=mesh,
        in_specs=placed,
        out_specs=(P("section", "dp", None, None, None),) * 4,
        check_vma=False,
    )
```
